256 devices in a mesh: comp: 2 (over x_lo), ox: 16 (over x_hi, y, core), oy: 8 (over z).
Axes of the slice: x: 4 (x_hi: 2, x_lo: 2; x = x_hi * 2 + x_lo), y: 4, z: 8, core: 2. Of those that a mesh axis runs over, the one named last changes fastest.
Arguments:
- atmos_stress: float32 [2, 2359296], P(None, ('comp', 'ox', 'oy')), may hold values from -6 to 6
- route_tile: int32 [2359296, 1], P(('comp', 'ox', 'oy')), may hold values from 0 to 255; in each aligned block of 9216 rows (0 to 9215, 9216 to 18431, ...) at most 144 rows name the same one
- route_cell: int32 [2359296], P(('comp', 'ox', 'oy')), may hold values from 0 to 54674
- route_weight: float32 [2359296], P(('comp', 'ox', 'oy')), may hold values from 0.25 to 1
- velocity: float32 [2, 8, 4320, 3240], P(None, None, ('comp', 'ox'), 'oy'), may hold values from -6 to 6
- thickness: float32 [8, 4320, 3240], P(None, ('comp', 'ox'), 'oy'), may hold values from 0.5 to 2
- coriolis: float32 [4320, 3240], P(('comp', 'ox'), 'oy'), may hold values from -0.5 to 0.5
- ocean_axes: float32 [2, 3, 4320, 3240], P(None, None, ('comp', 'ox'), 'oy'), may hold values from -3 to 3
- ocean_mask: int32 [4320, 3240], P(('comp', 'ox'), 'oy'), may hold values 0 or 1
Outputs:
- new_velocity: float32 [2, 8, 4320, 3240], P(None, None, ('comp', 'ox'), 'oy')
The draws below stay inside these ranges and needn't reach their ends.
Inputs may be any that keep to these rules, and one draw needn't show every extreme that they name: `route_tile`: tiles are numbered as devices, comp-major, then ox, then oy. Of the 9216 cells of one device, at most 144 name the same tile, and on some device exactly 144 do.
All inputs are finite; a program needn't handle non-finite values. No bound on the sum of `ocean_mask` on one device may be relied on, other than what follows from the above.
Results may differ from the reference program's by a relative error of at most 0.0003.
Values sent between devices are 32-bit elements; how exact they have to be, the bound alone decides.
A program may use at most 128 MiB of HBM per device.

```python
import math
import jax
import jax.numpy as jnp
import numpy as np
from jax import lax

A_ROWS = 48
A_COLS = 64
OX_DEV = 135
OY_DEV = 405
LEV = 8
FACES = 6
A_DEV = 9216
ATM_CELLS = 2359296
CAP = 144
NX = 4320
NY = 3240
O_DEV = 54675
N_COMP = 2
N_OX = 16
N_OY = 8
DEVICES = 256


def with_ends(entries, own_key, least, top_value):
    longest = entries.shape.index(max(entries.shape))
    spots = []
    for shift in (0, 1):
        where = [jax.random.randint(jax.random.fold_in(own_key, axis), (), 0, length) for axis, length in enumerate(entries.shape)]
        where[longest] = (where[longest] + shift) % entries.shape[longest]
        spots.append(tuple(where))
    return entries.at[spots[0]].set(least).at[spots[1]].set(top_value)


def steps_of(stream_key, dims, split, low, top_value):
    factor_of = 1.0
    for position, blocks in split:
        heights = jax.random.uniform(jax.random.fold_in(jax.random.fold_in(stream_key, 6), position), (blocks,), jnp.float32, low / len(split), top_value / len(split))
        factor_of = factor_of * jnp.repeat(jnp.exp(heights), dims[position] // blocks).reshape((-1,) + (1,) * (len(dims) - 1 - position))
    return factor_of


def shared_out(stream_key, own, number, rows, count, top, limit, slope):
    ranking = jax.random.permutation(stream_key, count)
    crowded, ordinary = shares(count, rows * top, limit, slope, True), shares(count, rows * top, limit, slope, False)
    places = jnp.arange(count)

    def named(lengths, offset_by):
        used = int((lengths > 0).sum())
        fixed = max(1, used // 4)
        moved = fixed + (places - fixed + offset_by * (used - fixed)) % max(1, count - fixed)
        return jnp.zeros((count,), jnp.int32).at[ranking[jnp.where(places < fixed, places, moved)]].set(jnp.asarray(lengths, jnp.int32))

    lengths = jnp.where(number % 4 == 0, named(crowded, number // 4), named(ordinary, number - number // 4 - 1))
    mixed = jax.random.permutation(jax.random.fold_in(own, 3), count)
    giver, taker = mixed[0:count // 2 * 2:2], mixed[1:count // 2 * 2:2]
    room = jnp.minimum(lengths[giver] - 1, limit - lengths[taker]) // 2
    room = jnp.where((giver == ranking[0]) | (taker == ranking[0]) | (lengths[taker] == 0), 0, jnp.maximum(room, 0))
    moved = jax.random.randint(jax.random.fold_in(own, 4), (count // 2,), 0, 1 << 20) % (room + 1)
    lengths = lengths.at[giver].add(-moved).at[taker].add(moved)
    items = jnp.searchsorted(jnp.cumsum(lengths), jnp.arange(rows * top), side="right").astype(jnp.int32)
    grid = items.reshape(top, rows).T
    grid = grid[jax.random.permutation(jax.random.fold_in(own, 1), rows)]
    offset_by = jax.random.randint(jax.random.fold_in(own, 2), (rows, 1), 0, top)
    return jnp.take_along_axis(grid, (jnp.arange(top)[None, :] + offset_by) % top, axis=1)


def shares(amount, total, limit, slope, full):
    weights = [(1 << 20) // math.isqrt(grade ** slope) + 1 for grade in range(1, amount + 1)]
    largest = limit if full else min(limit, max(-(-total // amount), total * weights[0] // sum(weights)))
    least = 1 if total - largest >= amount - 1 else 0
    holding, spare = [largest] + [least] * (amount - 1), total - largest - least * (amount - 1)
    while spare > 0:
        candidates = [i for i in range(1, amount) if holding[i] < largest] or [i for i in range(1, amount) if holding[i] < limit]
        whole, budget = sum([weights[i] for i in candidates]), spare
        for i in candidates:
            more = min(limit - holding[i], max(1, budget * weights[i] // whole), spare)
            holding[i] = holding[i] + more
            spare = spare - more
    return np.array(holding)


def gaussian(own_key, shape, width, limit, cuts=(), kind=jnp.bfloat16):
    values = width * jax.random.normal(own_key, shape, jnp.float32)
    if cuts:
        values = values * steps_of(own_key, shape, cuts, -0.22, 0.18)
    return jnp.clip(values, -limit, limit).astype(kind)


def setup_inputs(seed: int = 0) -> dict:
    streams_of = jax.random.split(jax.random.key(seed), 10)
    atmos_stress = gaussian(streams_of[0], (2, ATM_CELLS), 1.0, 6.0, ((1, 256),), jnp.float32)
    route_tile_keys = jax.random.split(jax.random.fold_in(streams_of[1], 1), ATM_CELLS // A_DEV)
    route_tile_turns = jax.random.permutation(jax.random.fold_in(streams_of[1], 3), ATM_CELLS // A_DEV)
    route_tile = jax.vmap(lambda own, number: shared_out(jax.random.fold_in(streams_of[1], 2), own, number, A_DEV, DEVICES, 1, CAP, 2))(route_tile_keys, route_tile_turns).reshape((ATM_CELLS, 1))
    route_cell = with_ends(jax.random.randint(streams_of[2], (ATM_CELLS,), 0, O_DEV), jax.random.fold_in(streams_of[2], 1), 0, O_DEV - 1).astype(jnp.int32)
    route_weight = jnp.clip(jnp.exp(math.log(1.0) - 1.3862944 * jax.random.uniform(streams_of[3], (ATM_CELLS,), jnp.float32) ** steps_of(streams_of[3], (ATM_CELLS,), ((0, 256),), -0.2, 0.2)), 0.25, 1.0)
    velocity = gaussian(streams_of[4], (2, LEV, NX, NY), 1.0, 6.0, ((2, 32), (3, 8)), jnp.float32)
    thickness = jnp.clip(jnp.exp(math.log(2.0) - 1.3862944 * jax.random.uniform(streams_of[5], (LEV, NX, NY), jnp.float32) ** steps_of(streams_of[5], (LEV, NX, NY), ((1, 32), (2, 8)), -0.2, 0.2)), 0.5, 2.0)
    coriolis = jnp.clip(jax.random.uniform(streams_of[6], (NX, NY), jnp.float32, -0.5, 0.5) * steps_of(streams_of[6], (NX, NY), ((0, 32), (1, 8)), -0.4, 0.0), -0.5, 0.5)
    ocean_axes = gaussian(streams_of[7], (2, 3, NX, NY), 0.6, 3.0, ((2, 32), (3, 8)), jnp.float32)
    ocean_mask = with_ends((jax.random.randint(streams_of[8], (NX, NY), 0, 5) < 4).astype(jnp.int32), jax.random.fold_in(streams_of[8], 1), 0, 1)
    return dict(atmos_stress=atmos_stress, route_tile=route_tile, route_cell=route_cell, route_weight=route_weight, velocity=velocity, thickness=thickness, coriolis=coriolis, ocean_axes=ocean_axes, ocean_mask=ocean_mask)


face_normal = np.array([[1.0, 0, 0], [0, 1.0, 0], [-1.0, 0, 0], [0, -1.0, 0], [0, 0, 1.0], [0, 0, -1.0]])
face_first = np.array([[0, 1.0, 0], [-1.0, 0, 0], [0, -1.0, 0], [1.0, 0, 0], [0, 1.0, 0], [0, 1.0, 0]])
face_second = np.array([[0, 0, 1.0], [0, 0, 1.0], [0, 0, 1.0], [0, 0, 1.0], [-1.0, 0, 0], [1.0, 0, 0]])
viscosity = 0.2
coupling = 0.3
bottom_drag = 0.1

def frame_rows(face_table, face_id):
    face_numbers = jnp.arange(6, dtype=jnp.int32)
    face_hits = (face_id[None, :] == face_numbers[:, None]).astype(jnp.float32)
    return jnp.dot(jnp.asarray(face_table.T, dtype=jnp.float32), face_hits, precision=lax.Precision.HIGHEST)

def tangent(direction, radial):
    projected = direction - lax.optimization_barrier(jnp.sum(direction * radial, axis=0, keepdims=True)) * radial
    return projected / jnp.sqrt(lax.optimization_barrier(jnp.sum(projected * projected, axis=0, keepdims=True)))

def cartesian(stress, face_id, cell_row, cell_col, cube_rows, cube_cols):
    normal = frame_rows(face_normal, face_id)
    first_axis = frame_rows(face_first, face_id)
    second_axis = frame_rows(face_second, face_id)
    slant_row = jnp.tan((cell_row.astype(jnp.float32) + 0.5) * (0.5 * math.pi / cube_rows) - 0.25 * math.pi)
    slant_col = jnp.tan((cell_col.astype(jnp.float32) + 0.5) * (0.5 * math.pi / cube_cols) - 0.25 * math.pi)
    surface_point = normal + slant_row[None, :] * first_axis + slant_col[None, :] * second_axis
    radial = surface_point / jnp.sqrt(lax.optimization_barrier(jnp.sum(surface_point * surface_point, axis=0, keepdims=True)))
    return stress[0][None, :] * tangent(first_axis, radial) + stress[1][None, :] * tangent(second_axis, radial)

def advance(masked, east, west, north, south, thickness, coriolis, ocean_stress, sea_mask):
    laplacian = east + west + north + south - 4.0 * masked
    turning = jnp.stack([coriolis * masked[1], -coriolis * masked[0]])
    interface_depth = 0.5 * (thickness[:-1] + thickness[1:])
    inner_flux = coupling * (masked[:, :-1] - masked[:, 1:]) / interface_depth[None]
    fluxes = jnp.concatenate([ocean_stress[:, None], inner_flux, bottom_drag * masked[:, -1:]], axis=1)
    vertical = (fluxes[:, :-1] - fluxes[:, 1:]) / thickness[None]
    return (masked + turning + viscosity * laplacian + vertical) * sea_mask

def reference(atmos_stress, route_tile, route_cell, route_weight, velocity, thickness, coriolis, ocean_axes, ocean_mask):
    cell_index = jnp.arange(ATM_CELLS, dtype=jnp.int32)
    device = cell_index // A_DEV
    local_index = cell_index % A_DEV
    half_index = device // (N_OX * N_OY)
    tile_row = device // N_OY % N_OX
    tile_col = device % N_OY
    face_id = half_index * (FACES // N_COMP) + local_index // (A_ROWS * A_COLS)
    cell_row = tile_row * A_ROWS + local_index // A_COLS % A_ROWS
    cell_col = tile_col * A_COLS + local_index % A_COLS
    weighted = cartesian(atmos_stress, face_id, cell_row, cell_col, A_ROWS * N_OX, A_COLS * N_OY) * route_weight[None, :]
    target = route_tile[:, 0]
    target_half = target // (N_OX * N_OY)
    target_x = target // N_OY % N_OX
    target_y = target % N_OY
    global_x = (target_half * N_OX + target_x) * OX_DEV + route_cell // OY_DEV
    global_y = target_y * OY_DEV + route_cell % OY_DEV
    flat_index = (global_x * NY + global_y).astype(jnp.int32)
    surface = jnp.zeros((3, NX * NY), jnp.float32).at[:, flat_index].add(weighted).reshape(3, NX, NY)
    ocean_stress = lax.optimization_barrier(jnp.sum(ocean_axes * surface[None], axis=1))
    sea_mask = ocean_mask.astype(jnp.float32)
    masked = velocity * sea_mask
    east = jnp.roll(masked, -1, axis=2)
    west = jnp.roll(masked, 1, axis=2)
    north = jnp.concatenate([masked[:, :, :, 1:], -masked[:, :, ::-1, -1:]], axis=3)
    south = jnp.concatenate([jnp.zeros_like(masked[:, :, :, :1]), masked[:, :, :, :-1]], axis=3)
    return advance(masked, east, west, north, south, thickness, coriolis, ocean_stress, sea_mask)
```

```python
import math

import jax
import jax.numpy as jnp
from jax import lax
from jax.experimental import pallas as pl
from jax.experimental.pallas import tpu as pltpu
from jax.sharding import PartitionSpec as P

BF = jnp.bfloat16
F32 = jnp.float32
I32 = jnp.int32
MESH = pl.DeviceIdType.MESH
FN=[[1,0,0],[0,1,0],[-1,0,0],[0,-1,0],[0,0,1],[0,0,-1]]
FA=[[0,1,0],[-1,0,0],[0,-1,0],[1,0,0],[0,1,0],[0,1,0]]
FB=[[0,0,1],[0,0,1],[0,0,1],[0,0,1],[-1,0,0],[1,0,0]]

def tan_small(t):
    u=t*t
    s=t*(1.0+u*(-1/6.0+u*(1/120.0+u*(-1/5040.0+u*(1/362880.0)))))
    c=1.0+u*(-0.5+u*(1/24.0+u*(-1/720.0+u*(1/40320.0+u*(-1/3628800.0)))))
    return s/c

def pack_kernel(pos_ref, stress_ref, tile_ref, cell_ref, weight_ref, out_ref, tout_ref, key_s, val_s, tr_s, sorted_s, start_v, start_s, tail_s, sem):
    comp=pos_ref[0]; ox=pos_ref[1]; oy=pos_ref[2]
    for f in range(3):
        rows=pl.ds(24*f,24)
        sub=lax.broadcasted_iota(I32,(24,128),0); lane=lax.broadcasted_iota(I32,(24,128),1)
        crow=ox*48+2*sub+lane//64
        ccol=oy*64+lane%64
        p=tan_small((crow.astype(F32)+0.5)*(0.5*math.pi/768)-0.25*math.pi)
        q=tan_small((ccol.astype(F32)+0.5)*(0.5*math.pi/512)-0.25*math.pi)
        pp=1.0+p*p; qq=1.0+q*q; rs=lax.rsqrt(pp+q*q)
        w=weight_ref[rows,:]*rs
        u=stress_ref[rows,0,:]*w*lax.rsqrt(qq)
        v=stress_ref[rows,1,:]*w*lax.rsqrt(pp)
        N=-(p*u+q*v); A=qq*u-p*q*v; B=pp*v-p*q*u
        for c in range(3):
            def coef(T): return jnp.where(comp==0,float(T[f][c]),float(T[f+3][c])).astype(F32)
            val_s[c,rows,:]=N*coef(FN)+A*coef(FA)+B*coef(FB)
    key_s[...]=tile_ref[...]*65536+cell_ref[...]
    tid=lax.broadcasted_iota(I32,(256,128),0)
    def cnt(r,acc):
        return acc+jnp.where(jnp.broadcast_to(tile_ref[pl.ds(r,1),:],(256,128))<tid,1.0,0.0)
    acc=lax.fori_loop(0,72,cnt,jnp.zeros((256,128),F32),unroll=8)
    st=lax.dot_general(jnp.ones((8,128),BF),acc.astype(BF),(((1,),(1,)),((),())),preferred_element_type=F32)
    start_v[...]=st.astype(I32)
    cp=pltpu.make_async_copy(start_v,start_s,sem); cp.start()
    keys=[key_s[pl.ds(8*i,8),:] for i in range(9)]+[jnp.full((8,128),2**31-1,I32)]*7
    vals=[[val_s[c,pl.ds(8*i,8),:] for i in range(9)]+[jnp.zeros((8,128),F32)]*7 for c in range(3)]
    lane=lax.broadcasted_iota(I32,(8,128),1); sub=lax.broadcasted_iota(I32,(8,128),0)
    arrs=[keys]+vals
    def bitmask(b):
        if b<4: return [bool((i>>b)&1) for i in range(16)]
        if b<7: return (sub>>(b-4))&1
        return (lane>>(b-7))&1
    for kk in range(1,15):
        for j in reversed(range(kk)):
            dirbits=bitmask(kk) if kk<14 else [False]*16
            if j<4:
                new=[[None]*16 for _ in arrs]
                for i in range(16):
                    if (i>>j)&1: continue
                    h=i|(1<<j)
                    a,b=arrs[0][i],arrs[0][h]
                    gt=a>b
                    if isinstance(dirbits,list):
                        swap=(b>a) if dirbits[i] else gt
                    else:
                        swap=jnp.where(dirbits==1,b-a,a-b)>0
                    for n in range(4):
                        x,y=arrs[n][i],arrs[n][h]
                        new[n][i]=jnp.where(swap,y,x); new[n][h]=jnp.where(swap,x,y)
                arrs=new
            else:
                bit=bitmask(j)
                if isinstance(dirbits,list): sgn=None
                new=[[None]*16 for _ in arrs]
                if j<7:
                    d=1<<(j-4)
                    part=lambda x: jnp.where(bit==1,pltpu.roll(x,d,0),pltpu.roll(x,8-d,0)) if d<4 else pltpu.roll(x,4,0)
                else:
                    d=1<<(j-7)
                    if d==64: part=lambda x: pltpu.roll(x,64,1)
                    else: part=lambda x: jnp.take_along_axis(x,lane^d,axis=1,mode="promise_in_bounds")
                for i in range(16):
                    k=arrs[0][i]; pk=part(k)
                    if isinstance(dirbits,list): flip=bit^(1 if dirbits[i] else 0)
                    else: flip=bit^dirbits
                    take=jnp.where(flip==1,pk-k,k-pk)>0
                    new[0][i]=jnp.where(take,pk,k)
                    for n in range(1,4):
                        x=arrs[n][i]
                        new[n][i]=jnp.where(take,part(x),x)
                arrs=new
    for n in range(4):
        for v in range(16):
            x=arrs[n][v]
            if n==0: x=(x&65535).astype(F32)
            tr_s[pl.ds(v,8,stride=16),:]=x
        t=tr_s[...].T
        sorted_s[:,(3 if n==0 else n-1),:]=t[:80]
    cp.wait()
    lane4=lax.broadcasted_iota(I32,(4,128),1); sub4=lax.broadcasted_iota(I32,(4,128),0)
    fill=jnp.where(sub4==3,-1.0,0.0).astype(F32)
    def put(t,_):
        s=start_s[0,t]
        e=jnp.where(t==255,9216,start_s[0,jnp.minimum(t+1,255)])
        n=e-s
        r=s//128; o=s%128
        sh=(128-o)%128
        x0,x1,x2=sorted_s[r],sorted_s[r+1],sorted_s[r+2]
        y0,y1,y2=[pltpu.roll(x,sh,1) for x in (x0,x1,x2)]
        inlo=lane4<128-o
        m=jnp.where(lane4<n,jnp.where(inlo,y0,y1),fill)
        g=jnp.where(lane4+128<n,jnp.where(inlo,y1,y2),fill)
        out_ref[t]=m
        tail_s[t]=g
        return 0
    lax.fori_loop(0,256,put,0,unroll=16)
    lane=lax.broadcasted_iota(I32,(256,128),1)
    tl=tail_s[:,3,:]
    tl=pltpu.roll(tl,48,1)
    for c in (2,1,0):
        g=tail_s[:,c,:]
        tl=jnp.where(lane<16*(c+1),pltpu.roll(g,16*c,1) if c else g,tl)
    tout_ref[:,0,:]=jnp.where(lane<64,tl,0.0)

W=80; SL=8; AR=304
def unpack_prepare(rec_ref, tail_ref, ent, mm_v):
    lane=lax.broadcasted_iota(I32,(256,128),1)
    tail=tail_ref[:,0,:]
    cellm=rec_ref[:,3,:]
    cellt=pltpu.roll(tail,80,1)
    n=jnp.sum(jnp.where(cellm>=0,1.0,0.0),axis=1,keepdims=True)+jnp.sum(jnp.where((cellt>=0)&(lane<16),1.0,0.0),axis=1,keepdims=True)
    S=jnp.maximum(jnp.max(n),1.0)
    def where_from(l):
        f=jnp.minimum(jnp.floor((l.astype(F32)*n+0.5)/S),143.0)
        g=jnp.minimum(jnp.floor(((l-1).astype(F32)*n+0.5)/S),143.0)
        return f,((f!=g)|(l==0))&(l.astype(F32)<S)&(n>0)
    fm,okm=where_from(lane)
    ft,okt=where_from(lane%16+128)
    fmi=jnp.clip(fm.astype(I32),0,127); fti=jnp.clip(ft.astype(I32),0,143)
    lo_i=jnp.minimum(fti,127)
    intail=fti>=128
    for c in (3,0,1,2):
        main=rec_ref[:,c,:]
        t=pltpu.roll(tail,(128-16*c)%128,1) if c else tail
        m2=jnp.take_along_axis(main,fmi,axis=1,mode="promise_in_bounds")
        ta=jnp.take_along_axis(main,lo_i,axis=1,mode="promise_in_bounds")
        tb=jnp.take_along_axis(t,jnp.where(intail,fti-128,0),axis=1,mode="promise_in_bounds")
        t2=jnp.where(intail,tb,ta)
        if c==3:
            m2=jnp.where(okm,m2,-1.0); t2=jnp.where(okt,t2,-1.0)
            for q,x in enumerate((m2,t2)):
                a=jnp.floor((x+0.5)*(1/256.0))
                mn=jnp.min(jnp.where(x>=0,a,999.0),axis=0,keepdims=True)
                mx=jnp.max(a,axis=0,keepdims=True)
                mm_v[pl.ds(0,1),pl.ds(128*q,128)]=mn.astype(I32)
                mm_v[pl.ds(1,1),pl.ds(128*q,128)]=mx.astype(I32)
        for x,r0,nr in ((m2,0,128),(t2,128,16)):
          for hh in range(2):
            y=x[128*hh:128*hh+128].T[:nr]
            rows=pl.ds(144*hh+r0,nr)
            if c==3:
                a=jnp.floor((y+0.5)*(1/256.0))
                ent[6,rows,:]=a
                ent[7,rows,:]=y-256.0*a
            else:
                h=y.astype(BF).astype(F32)
                ent[2*c,rows,:]=h
                ent[2*c+1,rows,:]=y-h
def unpack_chunks(ent, mm_s, surf, amat, bmat):
    R=2*SL
    ib=lax.broadcasted_iota(I32,(256,128),0).astype(F32).astype(BF)
    ia=lax.broadcasted_iota(I32,(W,128),0).astype(F32).astype(BF)
    one=jnp.ones((256,128),BF); zb=jnp.zeros((256,128),BF); za=jnp.zeros((W,128),BF)
    def row(k,j,h): return jnp.broadcast_to(ent[k,pl.ds(144*h+j,1),:],(16,128))
    def chunk(i,_):
        lo=mm_s[0,i*SL]; hi=mm_s[1,i*SL]
        for q in range(1,SL):
            lo=jnp.minimum(lo,mm_s[0,i*SL+q]); hi=jnp.maximum(hi,mm_s[1,i*SL+q])
        @pl.when(hi>=0)
        def _():
            for j in range(SL):
                for h in range(2):
                    bb=row(7,i*SL+j,h).astype(BF)
                    bmat[:,pl.ds((2*j+h)*128,128)]=jnp.where(ib==jnp.tile(bb,(16,1)),one,zb)
            base=(lo//8)*8
            def window(w,_):
                a0=pl.multiple_of(base+w*W,8)
                for j in range(SL):
                    for h in range(2):
                        ab=(row(6,i*SL+j,h)-a0.astype(F32)).astype(BF)
                        m=ia==jnp.tile(ab,(W//16,1))
                        for k in range(6):
                            v=row(k,i*SL+j,h).astype(BF)
                            amat[pl.ds(k*W,W),pl.ds((2*j+h)*128,128)]=jnp.where(m,jnp.tile(v,(W//16,1)),za)
                r=lax.dot_general(amat[...],bmat[...],(((1,),(1,)),((),())),preferred_element_type=F32)
                for c in range(3):
                    surf[c,pl.ds(a0,W),:]+=r[2*c*W:(2*c+1)*W]+r[(2*c+1)*W:(2*c+2)*W]
                return 0
            lax.fori_loop(0,(hi-base)//W+1,window,0)
        return 0
    lax.fori_loop(0,144//SL,chunk,0)
NXD,NYD=135,405

def edges(vel0, velr, row0, row1, mask_ref, xe_ref, ye_ref):
    for s,(row,x) in enumerate(((row0,0),(row1,NXD-1))):
        m=jnp.broadcast_to(mask_ref[x:x+1,:],(8,NYD)).astype(F32)
        for c in range(2): xe_ref[s,c]=row[c]*m
    ye_ref[...]=jnp.zeros_like(ye_ref)
    lane=lax.broadcasted_iota(I32,(8,128),1)
    def block(x0,n):
        ma=mask_ref[pl.ds(x0,n),0:1].astype(F32)
        mb=mask_ref[pl.ds(x0,n),NYD-1:NYD].astype(F32)
        for c in range(2):
            lo=jnp.zeros((8,128),F32); hi=lo; fold=lo
            for j in range(n):
                a=vel0[c,x0+j][:,0:1]*ma[j:j+1,:]
                b=velr[c,x0+j][:,20:21]*mb[j:j+1,:]
                lo=jnp.where(lane==j,a,lo); hi=jnp.where(lane==j,b,hi); fold=jnp.where(lane==6-j,-b,fold) if j<7 else jnp.where(lane==127,-b,fold)
            q=x0//128; o=x0%128
            ye_ref[0,c,q]+=pltpu.roll(lo,o,1); ye_ref[1,c,q]+=pltpu.roll(hi,o,1)
            f=pltpu.roll(fold,(256-x0)%128,1)
            tgt=(128-x0)+jnp.where(lane==127,-1,lane) if n==8 else None
            if isinstance(x0,int) and x0==0:
                ye_ref[2,c,1]+=jnp.where(lane<7,f,0.0); ye_ref[2,c,0]+=jnp.where(lane==127,f,0.0)
            else:
                ye_ref[2,c,0]+=f
    block(0,8)
    lax.fori_loop(1,16,lambda i,_:(block(pl.multiple_of(8*i,8),8),0)[1],0)
    block(128,7)

def stencil(vel, thick, cor, mask, xlo, xhi, ylo, yhi, south_scale, put, put_fac):
    sub=lax.broadcasted_iota(I32,(8,NYD),0)
    def mrow(M,j): return jnp.broadcast_to(M[j:j+1,:],(8,NYD))
    def block(x0,n,prev,cur,last):
        M=mask[pl.ds(x0,n),:].astype(F32); C=cor[pl.ds(x0,n),:]
        if not last:
            nxt0=pl.multiple_of(x0+8,8)
            Mn=mask[pl.ds(nxt0,7),:].astype(F32)
        q=x0//128; o=(128-x0%128)%128
        lo=[jnp.where(south_scale>0,pltpu.roll(ylo[c,q],o,1),0.0) for c in range(2)]
        hi=[pltpu.roll(yhi[c,q],o,1) for c in range(2)]
        for j in range(n):
            x=x0+j
            th=thick[x]; inv=1.0/th
            g=0.6/(th+pltpu.roll(th,7,0))
            m1=mrow(M,j); cj=mrow(C,j)
            put_fac(x,M[j:j+1,:]*inv[0:1,:])
            if last and j==n-1: nx=[xhi[c] for c in range(2)]
            else:
                mn=mrow(M,j+1) if j+1<n else mrow(Mn,0)
                nx=[vel[c,x+1]*mn for c in range(2)]
            for c in range(2):
                m=cur[c]
                north=jnp.concatenate([m[:,1:],hi[c][:,j:j+1]],axis=1)
                south=jnp.concatenate([lo[c][:,j:j+1],m[:,:-1]],axis=1)
                lap=(nx[c]+prev[c])+(north+south)-4.0*m
                D=jnp.where(sub==7,0.1*m,g*(m-pltpu.roll(m,7,0)))
                ab=jnp.where(sub==0,0.0,pltpu.roll(D,1,0))
                turn=cj*cur[1] if c==0 else -cj*cur[0]
                put(c,x,(m+turn+0.2*lap+(ab-D)*inv)*m1)
            prev,cur=cur,nx
        return prev,cur
    m0=jnp.broadcast_to(mask[0:1,:],(8,NYD)).astype(F32)
    prev=[xlo[c] for c in range(2)]; cur=[vel[c,0]*m0 for c in range(2)]
    def body(i,st):
        p,c=block(pl.multiple_of(8*i,8),8,list(st[0]),list(st[1]),False)
        return tuple(p),tuple(c)
    st=lax.fori_loop(0,16,body,(tuple(prev),tuple(cur)))
    block(128,7,list(st[0]),list(st[1]),True)

def stencil_kernel(pos_ref,vel,thick,cor,mask,xh,yh,out,fac):
    ss=jnp.where(pos_ref[2]==0,0.0,1.0).astype(F32)
    def put(c,x,v): out[c,x]=v
    def put_fac(x,v): fac[x]=jnp.broadcast_to(v,(2,NYD))
    stencil(vel,thick,cor,mask,xh.at[0],xh.at[1],yh.at[0],yh.at[1],ss,put,put_fac)
V=pl.BlockSpec(memory_space=pltpu.VMEM); SM=pl.BlockSpec(memory_space=pltpu.SMEM)

def pack_edge_kernel(pos_ref, stress_ref, tile_ref, cell_ref, weight_ref, vel_hbm, mask_ref, out_ref, tout_ref, xe_ref, ye_ref,
                     key_s, val_s, tr_s, sorted_s, start_v, start_s, tail_s, vel0, velr, row0, row1, sem, esem):
    copies = [
        pltpu.make_async_copy(vel_hbm.at[:, :, :, 0:128], vel0, esem.at[0]),
        pltpu.make_async_copy(vel_hbm.at[:, :, :, 384:405], velr, esem.at[1]),
        pltpu.make_async_copy(vel_hbm.at[:, 0], row0, esem.at[2]),
        pltpu.make_async_copy(vel_hbm.at[:, NXD - 1], row1, esem.at[3]),
    ]
    for copy in copies:
        copy.start()
    pack_kernel(pos_ref, stress_ref, tile_ref, cell_ref, weight_ref, out_ref, tout_ref,
                key_s, val_s, tr_s, sorted_s, start_v, start_s, tail_s, sem)
    for copy in copies:
        copy.wait()
    edges(vel0, velr, row0, row1, mask_ref, xe_ref, ye_ref)


V = pl.BlockSpec(memory_space=pltpu.VMEM)
SM = pl.BlockSpec(memory_space=pltpu.SMEM)
ANY = pl.BlockSpec(memory_space=pl.ANY)


def pack_edge(pos, stress, tile, cell, weight, vel, mask):
    st = stress.reshape(2, 72, 128).transpose(1, 0, 2)
    return pl.pallas_call(
        pack_edge_kernel,
        out_shape=(
            jax.ShapeDtypeStruct((256, 4, 128), F32),
            jax.ShapeDtypeStruct((256, 1, 128), F32),
            jax.ShapeDtypeStruct((2, 2, 8, NYD), F32),
            jax.ShapeDtypeStruct((3, 2, 2, 8, 128), F32),
        ),
        in_specs=[SM, V, V, V, V, ANY, V],
        out_specs=(V, V, V, V),
        scratch_shapes=[
            pltpu.VMEM((72, 128), I32), pltpu.VMEM((3, 72, 128), F32), pltpu.VMEM((128, 128), F32),
            pltpu.VMEM((80, 4, 128), F32), pltpu.VMEM((8, 256), I32), pltpu.SMEM((8, 256), I32),
            pltpu.VMEM((256, 4, 128), F32),
            pltpu.VMEM((2, NXD, 8, 128), F32), pltpu.VMEM((2, NXD, 8, 21), F32),
            pltpu.VMEM((2, 8, NYD), F32), pltpu.VMEM((2, 8, NYD), F32),
            pltpu.SemaphoreType.DMA, pltpu.SemaphoreType.DMA((4,)),
        ],
        compiler_params=pltpu.CompilerParams(vmem_limit_bytes=30 << 20),
    )(pos, st, tile.reshape(72, 128), cell.reshape(72, 128), weight.reshape(72, 128), vel, mask)


def coords(d):
    return d // 128, d // 8 % 16, d % 8


def exchange_kernel(main, tail, xe, ye, rec, rtail, xh, yh, lsem, ssem, rsem, xs, xr, ys, yr):
    comp, ox, oy = lax.axis_index("comp"), lax.axis_index("ox"), lax.axis_index("oy")
    me = comp * 128 + ox * 8 + oy
    p = comp * 16 + ox
    barrier = pltpu.get_barrier_semaphore()

    def greet(i, carry):
        pl.semaphore_signal(barrier, inc=1, device_id=coords((me + i) % 256), device_id_type=MESH)
        return carry

    lax.fori_loop(1, 256, greet, 0)
    own = [
        pltpu.make_async_copy(main.at[me], rec.at[me], lsem.at[0]),
        pltpu.make_async_copy(tail.at[me], rtail.at[me], lsem.at[1]),
    ]
    for copy in own:
        copy.start()
    pl.semaphore_wait(barrier, 255)

    def remote(src, dst, ss, rs, pp, oyy):
        return pltpu.make_async_remote_copy(
            src_ref=src, dst_ref=dst, send_sem=ss, recv_sem=rs,
            device_id=(pp // 16, pp % 16, oyy), device_id_type=MESH)

    west, east = (p + 31) % 32, (p + 1) % 32
    x_low = remote(xe.at[0], xh.at[1], xs.at[0], xr.at[1], west, oy)
    x_high = remote(xe.at[1], xh.at[0], xs.at[1], xr.at[0], east, oy)
    y_low = remote(ye.at[0], yh.at[1], ys.at[0], yr.at[1], p, (oy + 7) % 8)
    y_high = remote(ye.at[1], yh.at[0], ys.at[1], yr.at[0], p, (oy + 1) % 8)
    fold = remote(ye.at[2], yh.at[1], ys.at[2], yr.at[1], 31 - p, oy)
    x_low.start()
    x_high.start()

    @pl.when(oy > 0)
    def _():
        y_low.start()

    @pl.when(oy < 7)
    def _():
        y_high.start()

    @pl.when(oy == 7)
    def _():
        fold.start()

    def send(i, carry):
        d = (me + i) % 256
        dev = coords(d)
        pltpu.make_async_remote_copy(
            src_ref=main.at[d], dst_ref=rec.at[me], send_sem=ssem.at[0], recv_sem=rsem.at[0],
            device_id=dev, device_id_type=MESH).start()
        pltpu.make_async_remote_copy(
            src_ref=tail.at[d], dst_ref=rtail.at[me], send_sem=ssem.at[1], recv_sem=rsem.at[1],
            device_id=dev, device_id_type=MESH).start()
        return carry

    lax.fori_loop(1, 256, send, 0)
    for copy in own:
        copy.wait()
    x_low.wait()
    x_high.wait()

    @pl.when(oy > 0)
    def _():
        y_low.wait_send()
        pltpu.make_async_copy(ye.at[1], yh.at[0], yr.at[0]).wait()

    @pl.when(oy < 7)
    def _():
        y_high.wait_send()

    @pl.when(oy == 7)
    def _():
        fold.wait_send()

    pltpu.make_async_copy(ye.at[0], yh.at[1], yr.at[1]).wait()
    n = pl.ds(0, 255)
    pltpu.make_async_copy(main.at[n], rec.at[n], ssem.at[0]).wait()
    pltpu.make_async_copy(tail.at[n], rtail.at[n], ssem.at[1]).wait()
    pltpu.make_async_copy(main.at[n], rec.at[n], rsem.at[0]).wait()
    pltpu.make_async_copy(tail.at[n], rtail.at[n], rsem.at[1]).wait()


def exchange(main, tail, xe, ye):
    shapes = [jax.ShapeDtypeStruct(a.shape, a.dtype) for a in (main, tail, xe)]
    shapes.append(jax.ShapeDtypeStruct((2, 2, 2, 8, 128), F32))
    D = pltpu.SemaphoreType.DMA
    return pl.pallas_call(
        exchange_kernel,
        out_shape=tuple(shapes),
        in_specs=[ANY] * 4,
        out_specs=(ANY,) * 4,
        scratch_shapes=[D((2,)), D((2,)), D((2,)), D((2,)), D((2,)), D((3,)), D((2,))],
        compiler_params=pltpu.CompilerParams(collective_id=0, has_side_effects=True),
    )(main, tail, xe, ye)


def step_kernel(pos_ref, vel, thick, cor, mask, xh, yh, out, fac):
    stencil_kernel(pos_ref, vel, thick, cor, mask, xh, yh, out, fac)


def momentum(pos, vel, thick, cor, mask, xh, yh):
    return pl.pallas_call(
        step_kernel,
        out_shape=(jax.ShapeDtypeStruct((2, NXD, 8, NYD), F32), jax.ShapeDtypeStruct((NXD, 2, NYD), F32)),
        in_specs=[SM] + [V] * 6,
        out_specs=(V, V),
        compiler_params=pltpu.CompilerParams(vmem_limit_bytes=40 << 20),
    )(pos, vel, thick, cor, mask, xh, yh)


ROWS = 15


def finish_kernel(rec, rtail, step_hbm, axes_hbm, fac_hbm, out_hbm, ent, mm_v, mm_s, amat, bmat, surf, flat, step, axes, fac, sem, isem, osem):
    loads = [
        pltpu.make_async_copy(step_hbm, step, isem.at[0]),
        pltpu.make_async_copy(axes_hbm, axes, isem.at[1]),
        pltpu.make_async_copy(fac_hbm, fac, isem.at[2]),
    ]
    for copy in loads:
        copy.start()
    unpack_prepare(rec, rtail, ent, mm_v)
    copy = pltpu.make_async_copy(mm_v, mm_s, sem)
    copy.start()
    surf[...] = jnp.zeros_like(surf)
    copy.wait()
    unpack_chunks(ent, mm_s, surf, amat, bmat)
    for c in range(3):
        for h in range(2):
            flat[pl.ds(h, 216, stride=2), c, :] = surf[c, 0:216, 128 * h:128 * h + 128]
    for copy in loads:
        copy.wait()

    def row(x):
        r, o = 405 * x // 128, 405 * x % 128
        lane = lax.broadcasted_iota(I32, (4, 128), 1)
        t = [pltpu.roll(flat[r + k], (128 - o) % 128, 1) for k in range(5)]
        cut = lane < 128 - o
        for q in range(4):
            w = min(128, NYD - 128 * q)
            s = jnp.where(cut, t[q], t[q + 1])
            cols = pl.ds(128 * q, w)
            total = jnp.zeros((2, w), F32)
            for c in range(3):
                total += axes[c, x, :, cols] * jnp.broadcast_to(s[c:c + 1, :w], (2, w))
            total = total * fac[x, :, cols]
            for i in range(2):
                step[i, x, 0:1, cols] += total[i:i + 1, :]

    def out_copy(g):
        rows = pl.ds(g * ROWS, ROWS)
        return pltpu.make_async_copy(step.at[:, rows], out_hbm.at[:, rows], osem.at[g])

    def group(g, carry):
        def one(k, carry):
            row(g * ROWS + k)
            return carry

        lax.fori_loop(0, ROWS, one, 0, unroll=3)
        out_copy(g).start()
        return carry

    lax.fori_loop(0, NXD // ROWS, group, 0)

    def drain(g, carry):
        out_copy(g).wait()
        return carry

    lax.fori_loop(0, NXD // ROWS, drain, 0)


def finish(rec, rtail, step, axes, fac):
    D = pltpu.SemaphoreType.DMA
    return pl.pallas_call(
        finish_kernel,
        out_shape=jax.ShapeDtypeStruct((2, NXD, 8, NYD), F32),
        in_specs=[V, V, ANY, ANY, ANY],
        out_specs=ANY,
        scratch_shapes=[
            pltpu.VMEM((8, 288, 128), F32), pltpu.VMEM((8, 256), I32), pltpu.SMEM((8, 256), I32),
            pltpu.VMEM((6 * W, SL * 256), BF), pltpu.VMEM((256, SL * 256), BF),
            pltpu.VMEM((3, AR, 256), F32), pltpu.VMEM((432, 4, 128), F32),
            pltpu.VMEM((2, NXD, 8, NYD), F32), pltpu.VMEM((3, NXD, 2, NYD), F32), pltpu.VMEM((NXD, 2, NYD), F32),
            D, D((3,)), D((NXD // ROWS,)),
        ],
        compiler_params=pltpu.CompilerParams(vmem_limit_bytes=50 << 20),
    )(rec, rtail, step, axes, fac)


def shards(atmos_stress, route_tile, route_cell, route_weight, velocity, thickness, coriolis, ocean_axes, ocean_mask):
    pos = jnp.stack([lax.axis_index("comp"), lax.axis_index("ox"), lax.axis_index("oy")]).astype(I32)
    vel = velocity.transpose(0, 2, 1, 3)
    main, tail, xe, ye = pack_edge(pos, atmos_stress, route_tile, route_cell, route_weight, vel, ocean_mask)
    rec, rtail, xh, yh = exchange(main, tail, xe, ye)
    step, fac = momentum(pos, vel, thickness.transpose(1, 0, 2), coriolis, ocean_mask, xh, yh)
    out = finish(rec, rtail, step, ocean_axes.transpose(1, 2, 0, 3), fac)
    return out.transpose(0, 2, 1, 3)


def solution(mesh):
    return jax.shard_map(
        shards,
        mesh=mesh,
        in_specs=(
            P(None, ("comp", "ox", "oy")),
            P(("comp", "ox", "oy"), None),
            P(("comp", "ox", "oy")),
            P(("comp", "ox", "oy")),
            P(None, None, ("comp", "ox"), "oy"),
            P(None, ("comp", "ox"), "oy"),
            P(("comp", "ox"), "oy"),
            P(None, None, ("comp", "ox"), "oy"),
            P(("comp", "ox"), "oy"),
        ),
        out_specs=P(None, None, ("comp", "ox"), "oy"),
        check_vma=False,
    )
```

```python
import math

import jax
import jax.numpy as jnp
from jax import lax
from jax.experimental import pallas as pl
from jax.experimental.pallas import tpu as pltpu
from jax.sharding import PartitionSpec as P

BF = jnp.bfloat16
F32 = jnp.float32
I32 = jnp.int32
MESH = pl.DeviceIdType.MESH
FN=[[1,0,0],[0,1,0],[-1,0,0],[0,-1,0],[0,0,1],[0,0,-1]]
FA=[[0,1,0],[-1,0,0],[0,-1,0],[1,0,0],[0,1,0],[0,1,0]]
FB=[[0,0,1],[0,0,1],[0,0,1],[0,0,1],[-1,0,0],[1,0,0]]

def tan_small(t):
    u=t*t
    s=t*(1.0+u*(-1/6.0+u*(1/120.0+u*(-1/5040.0+u*(1/362880.0)))))
    c=1.0+u*(-0.5+u*(1/24.0+u*(-1/720.0+u*(1/40320.0+u*(-1/3628800.0)))))
    return s/c

def pack_kernel(pos_ref, stress_ref, tile_ref, cell_ref, weight_ref, out_ref, tout_ref, key_s, val_s, tr_s):
    comp=pos_ref[0]; ox=pos_ref[1]; oy=pos_ref[2]
    for f in range(3):
        rows=pl.ds(24*f,24)
        sub=lax.broadcasted_iota(I32,(24,128),0); lane=lax.broadcasted_iota(I32,(24,128),1)
        crow=ox*48+2*sub+lane//64
        ccol=oy*64+lane%64
        p=tan_small((crow.astype(F32)+0.5)*(0.5*math.pi/768)-0.25*math.pi)
        q=tan_small((ccol.astype(F32)+0.5)*(0.5*math.pi/512)-0.25*math.pi)
        pp=1.0+p*p; qq=1.0+q*q; rs=lax.rsqrt(pp+q*q)
        w=weight_ref[rows,:]*rs
        u=stress_ref[rows,0,:]*w*lax.rsqrt(qq)
        v=stress_ref[rows,1,:]*w*lax.rsqrt(pp)
        N=-(p*u+q*v); A=qq*u-p*q*v; B=pp*v-p*q*u
        for c in range(3):
            def coef(T): return jnp.where(comp==0,float(T[f][c]),float(T[f+3][c])).astype(F32)
            val_s[c,rows,:]=N*coef(FN)+A*coef(FA)+B*coef(FB)
    key_s[...]=tile_ref[...]*65536+cell_ref[...]
    tid=lax.broadcasted_iota(I32,(256,128),0)
    def cnt(r,acc):
        rows=tile_ref[pl.ds(pl.multiple_of(8*r,8),8),:]
        for k in range(8):
            acc=acc+jnp.where(jnp.broadcast_to(rows[k:k+1,:],(256,128))<tid,1.0,0.0)
        return acc
    acc=lax.fori_loop(0,9,cnt,jnp.zeros((256,128),F32))
    start=jnp.sum(acc,axis=1,keepdims=True)
    keys=[key_s[pl.ds(8*i,8),:] for i in range(9)]+[jnp.full((8,128),2**31-1,I32)]*7
    vals=[[val_s[c,pl.ds(8*i,8),:] for i in range(9)]+[jnp.zeros((8,128),F32)]*7 for c in range(3)]
    lane=lax.broadcasted_iota(I32,(8,128),1); sub=lax.broadcasted_iota(I32,(8,128),0)
    arrs=[keys]+vals
    def bitmask(b):
        if b<3: return (sub>>b)&1
        if b<7: return [bool((i>>(b-3))&1) for i in range(16)]
        return (lane>>(b-7))&1
    for kk in range(1,15):
        for j in reversed(range(kk)):
            dirbits=bitmask(kk) if kk<14 else [False]*16
            if 3<=j<7:
                new=[[None]*16 for _ in arrs]
                for i in range(16):
                    if (i>>(j-3))&1: continue
                    h=i|(1<<(j-3))
                    a,b=arrs[0][i],arrs[0][h]
                    gt=a>b
                    if isinstance(dirbits,list):
                        swap=(b>a) if dirbits[i] else gt
                    else:
                        swap=jnp.where(dirbits==1,b-a,a-b)>0
                    for n in range(4):
                        x,y=arrs[n][i],arrs[n][h]
                        new[n][i]=jnp.where(swap,y,x); new[n][h]=jnp.where(swap,x,y)
                arrs=new
            else:
                bit=bitmask(j)
                if isinstance(dirbits,list): sgn=None
                new=[[None]*16 for _ in arrs]
                if j<3:
                    d=1<<j
                    part=lambda x: jnp.where(bit==1,pltpu.roll(x,d,0),pltpu.roll(x,8-d,0)) if d<4 else pltpu.roll(x,4,0)
                else:
                    d=1<<(j-7)
                    if d==64: part=lambda x: pltpu.roll(x,64,1)
                    else: part=lambda x: jnp.take_along_axis(x,lane^d,axis=1,mode="promise_in_bounds")
                for i in range(16):
                    k=arrs[0][i]; pk=part(k)
                    if isinstance(dirbits,list): flip=bit^(1 if dirbits[i] else 0)
                    else: flip=bit^dirbits
                    take=jnp.where(flip==1,pk-k,k-pk)>0
                    new[0][i]=jnp.where(take,pk,k)
                    for n in range(1,4):
                        x=arrs[n][i]
                        new[n][i]=jnp.where(take,part(x),x)
                arrs=new
    turned=[None]*4
    for n in range(4):
        for v in range(16):
            x=arrs[n][v]
            if n==0: x=(x&65535).astype(F32)
            tr_s[pl.ds(8*v,8),:]=x
        turned[3 if n==0 else n-1]=tr_s[...].T
    table=jnp.concatenate(turned,axis=1)
    p0=table.astype(BF); d0=table-p0.astype(F32)
    p1=d0.astype(BF); p2=(d0-p1.astype(F32)).astype(BF)
    lane=lax.broadcasted_iota(I32,(256,128),1).astype(F32)
    start=jnp.broadcast_to(start,(256,128))
    row=jnp.floor(start*(1.0/128)); off=start-128.0*row
    last=lax.broadcasted_iota(I32,(256,128),0)==255
    left=jnp.where(last,9216.0,pltpu.roll(start,255,0))-start
    got=[]
    for k in range(3):
        pick=jnp.where(lane==row+float(k),1.0,0.0).astype(BF)
        got.append(sum(jnp.dot(pick,q,preferred_element_type=F32) for q in (p0,p1,p2)))
    at=(lane+off).astype(I32)&127
    inlo=lane+off<128.0
    tl=jnp.zeros((256,128),F32)
    for c in range(4):
        y0,y1,y2=[jnp.take_along_axis(g[:,128*c:128*c+128],at,axis=1,mode="promise_in_bounds") for g in got]
        fill=-1.0 if c==3 else 0.0
        out_ref[:,c,:]=jnp.where(lane<left,jnp.where(inlo,y0,y1),fill)
        g=jnp.where(lane+128.0<left,jnp.where(inlo,y1,y2),fill)
        if c: g=pltpu.roll(g,16*c,1)
        tl=jnp.where((lane>=16.0*c)&(lane<16.0*c+16.0),g,tl)
    tout_ref[:,0,:]=tl

W=80; SL=8; AR=304
def unpack_prepare(rec_ref, tail_ref, ent, mm_v):
    lane=lax.broadcasted_iota(I32,(256,128),1)
    tail=tail_ref[:,0,:]
    cellm=rec_ref[:,3,:]
    cellt=pltpu.roll(tail,80,1)
    n=jnp.sum(jnp.where(cellm>=0,1.0,0.0),axis=1,keepdims=True)+jnp.sum(jnp.where((cellt>=0)&(lane<16),1.0,0.0),axis=1,keepdims=True)
    S=jnp.maximum(jnp.max(n),1.0)
    def where_from(l):
        f=jnp.minimum(jnp.floor((l.astype(F32)*n+0.5)/S),143.0)
        g=jnp.minimum(jnp.floor(((l-1).astype(F32)*n+0.5)/S),143.0)
        return f,((f!=g)|(l==0))&(l.astype(F32)<S)&(n>0)
    fm,okm=where_from(lane)
    ft,okt=where_from(lane%16+128)
    fmi=jnp.clip(fm.astype(I32),0,127); fti=jnp.clip(ft.astype(I32),0,143)
    lo_i=jnp.minimum(fti,127)
    intail=fti>=128
    for c in (3,0,1,2):
        main=rec_ref[:,c,:]
        t=pltpu.roll(tail,(128-16*c)%128,1) if c else tail
        m2=jnp.take_along_axis(main,fmi,axis=1,mode="promise_in_bounds")
        ta=jnp.take_along_axis(main,lo_i,axis=1,mode="promise_in_bounds")
        tb=jnp.take_along_axis(t,jnp.where(intail,fti-128,0),axis=1,mode="promise_in_bounds")
        t2=jnp.where(intail,tb,ta)
        if c==3:
            m2=jnp.where(okm,m2,-1.0); t2=jnp.where(okt,t2,-1.0)
            for q,x in enumerate((m2,t2)):
                a=jnp.floor((x+0.5)*(1/256.0))
                mn=jnp.min(jnp.where(x>=0,a,999.0),axis=0,keepdims=True)
                mx=jnp.max(a,axis=0,keepdims=True)
                mm_v[pl.ds(0,1),pl.ds(128*q,128)]=mn.astype(I32)
                mm_v[pl.ds(1,1),pl.ds(128*q,128)]=mx.astype(I32)
        for x,r0,nr in ((m2,0,128),(t2,128,16)):
          for hh in range(2):
            y=x[128*hh:128*hh+128].T[:nr]
            rows=pl.ds(144*hh+r0,nr)
            if c==3:
                a=jnp.floor((y+0.5)*(1/256.0))
                ent[6,rows,:]=a
                ent[7,rows,:]=y-256.0*a
            else:
                h=y.astype(BF).astype(F32)
                ent[2*c,rows,:]=h
                ent[2*c+1,rows,:]=y-h
def unpack_chunks(ent, mm_s, surf, amat0, amat1, bmat0, bmat1, jobs):
    ib=lax.broadcasted_iota(I32,(256,128),0).astype(F32).astype(BF)
    ia=lax.broadcasted_iota(I32,(W,128),0).astype(F32).astype(BF)
    one=jnp.ones((256,128),BF); zb=jnp.zeros((256,128),BF); za=jnp.zeros((W,128),BF)
    def row(k,j,h): return jnp.broadcast_to(ent[k,pl.ds(144*h+j,1),:],(16,128))
    def chunk(i,n):
        lo=mm_s[0,i*SL]; hi=mm_s[1,i*SL]
        for q in range(1,SL):
            lo=jnp.minimum(lo,mm_s[0,i*SL+q]); hi=jnp.maximum(hi,mm_s[1,i*SL+q])
        base=(lo//8)*8
        def add(w,n):
            jobs[0,n]=i
            jobs[1,n]=base+w*W
            return n+1
        return lax.fori_loop(0,jnp.where(hi>=0,(hi-base)//W+1,0),add,n)
    n=lax.fori_loop(0,144//SL,chunk,0)
    for k in range(3):
        jobs[0,n+k]=0
        jobs[1,n+k]=AR-W
    def make(k,amat,bmat):
        i=jobs[0,k]; a0=jobs[1,k].astype(F32)
        for j in range(SL):
            for h in range(2):
                cols=pl.ds((2*j+h)*128,128)
                bb=row(7,i*SL+j,h).astype(BF)
                bmat[:,cols]=jnp.where(ib==jnp.tile(bb,(16,1)),one,zb)
                ab=(row(6,i*SL+j,h)-a0).astype(BF)
                m=ia==jnp.tile(ab,(W//16,1))
                for q in range(6):
                    v=row(q,i*SL+j,h).astype(BF)
                    amat[pl.ds(q*W,W),cols]=jnp.where(m,jnp.tile(v,(W//16,1)),za)
    def add_product(k,amat,bmat):
        a0=pl.multiple_of(jobs[1,k],8)
        r=lax.dot_general(amat[...],bmat[...],(((1,),(1,)),((),())),preferred_element_type=F32)
        for c in range(3):
            surf[c,pl.ds(a0,W),:]+=r[2*c*W:(2*c+1)*W]+r[(2*c+1)*W:(2*c+2)*W]
    make(0,amat0,bmat0)
    def pair(t,carry):
        make(2*t+1,amat1,bmat1)
        add_product(2*t,amat0,bmat0)
        make(2*t+2,amat0,bmat0)
        add_product(2*t+1,amat1,bmat1)
        return carry
    lax.fori_loop(0,(n+1)//2,pair,0)
NXD,NYD=135,405

def edges(vel, mask_ref, xe_ref, ye_ref):
    for s,x in ((0,0),(1,NXD-1)):
        M=mask_ref[0:8,:] if s==0 else mask_ref[NXD-8:NXD,:]
        j=0 if s==0 else 7
        m=jnp.broadcast_to(M[j:j+1,:],(8,NYD)).astype(F32)
        for c in range(2): xe_ref[s,c]=vel[c,x]*m
    ye_ref[...]=jnp.zeros_like(ye_ref)
    lane=lax.broadcasted_iota(I32,(8,128),1)
    def block(x0,first,M):
        ma=M[:,0:1]; mb=M[:,NYD-1:NYD]
        static=isinstance(x0,int)
        q=x0//128 if static else 0
        o=x0%128
        for c in range(2):
            lo=jnp.zeros((8,128),F32); hi=lo; fold=lo
            for j in range(first,8):
                v=vel[c,x0+j]
                a=v[:,0:1]*ma[j:j+1,:]
                b=v[:,NYD-1:NYD]*mb[j:j+1,:]
                lo=jnp.where(lane==j,a,lo); hi=jnp.where(lane==j,b,hi); fold=jnp.where(lane==7-j,-b,fold)
            f=pltpu.roll(fold,(127-x0)%128 if static else (127-x0),1)
            lo=pltpu.roll(lo,o,1); hi=pltpu.roll(hi,o,1)
            if static and x0==127:
                ye_ref[0,c,1]=jnp.where(lane<7,lo,0.0); ye_ref[1,c,1]=jnp.where(lane<7,hi,0.0)
                ye_ref[2,c,0]+=f
            elif static and x0==0:
                ye_ref[0,c,0]+=lo; ye_ref[1,c,0]+=hi
                ye_ref[2,c,1]+=jnp.where(lane<7,f,0.0); ye_ref[2,c,0]+=jnp.where(lane==127,f,0.0)
            else:
                ye_ref[0,c,0]+=lo; ye_ref[1,c,0]+=hi; ye_ref[2,c,0]+=f
    def rows(x0): return mask_ref[pl.ds(x0,8),:].astype(F32)
    block(0,0,rows(0))
    def body(i,carry):
        x0=pl.multiple_of(8*i,8)
        block(x0,0,rows(x0))
        return carry
    lax.fori_loop(1,16,body,0)
    block(127,1,mask_ref[NXD-8:NXD,:].astype(F32))

def stencil(vel, thick, cor, mask, xlo, xhi, ylo, yhi, south_scale, put, put_fac):
    sub=lax.broadcasted_iota(I32,(8,NYD),0)
    def mrow(M,j): return jnp.broadcast_to(M[j:j+1,:],(8,NYD))
    def rows8(ref,x0): return ref[pl.ds(x0,8),:].astype(F32)
    M_end=mask[NXD-8:NXD,:].astype(F32)[1:8]; C_end=cor[NXD-8:NXD,:][1:8]
    def block(x0,n,prev,cur,last):
        M=M_end if last else rows8(mask,x0); C=C_end if last else rows8(cor,x0)
        if not last:
            Mn=M_end if isinstance(x0,int) else rows8(mask,pl.multiple_of(x0+8,8))
        q=x0//128 if isinstance(x0,int) else 0
        o=(128-x0%128)%128
        lo=[jnp.where(south_scale>0,pltpu.roll(ylo[c,q],o,1),0.0) for c in range(2)]
        hi=[pltpu.roll(yhi[c,q],o,1) for c in range(2)]
        for j in range(n):
            x=x0+j
            th=thick[x]; inv=1.0/th
            g=0.6/(th+pltpu.roll(th,7,0))
            m1=mrow(M,j); cj=mrow(C,j)
            put_fac(x,M[j:j+1,:]*inv[0:1,:])
            if last and j==n-1: nx=[xhi[c] for c in range(2)]
            else:
                mn=mrow(M,j+1) if j+1<n else mrow(Mn,0)
                nx=[vel[c,x+1]*mn for c in range(2)]
            for c in range(2):
                m=cur[c]
                north=jnp.concatenate([m[:,1:],hi[c][:,j:j+1]],axis=1)
                south=jnp.concatenate([lo[c][:,j:j+1],m[:,:-1]],axis=1)
                lap=(nx[c]+prev[c])+(north+south)-4.0*m
                D=jnp.where(sub==7,0.1*m,g*(m-pltpu.roll(m,7,0)))
                ab=jnp.where(sub==0,0.0,pltpu.roll(D,1,0))
                turn=cj*cur[1] if c==0 else -cj*cur[0]
                put(c,x,(m+turn+0.2*lap+(ab-D)*inv)*m1)
            prev,cur=cur,nx
        return prev,cur
    m0=jnp.broadcast_to(rows8(mask,0)[0:1,:],(8,NYD))
    prev=[xlo[c] for c in range(2)]; cur=[vel[c,0]*m0 for c in range(2)]
    def body(i,st):
        p,c=block(pl.multiple_of(8*i,8),8,list(st[0]),list(st[1]),False)
        return tuple(p),tuple(c)
    st=lax.fori_loop(0,15,body,(tuple(prev),tuple(cur)))
    st=block(120,8,list(st[0]),list(st[1]),False)
    block(128,7,list(st[0]),list(st[1]),True)

def stencil_kernel(pos_ref,vel,thick,cor,mask,xh,yh,out,fac):
    ss=jnp.where(pos_ref[2]==0,0.0,1.0).astype(F32)
    def put(c,x,v): out[c,x]=v
    def put_fac(x,v): fac[x]=jnp.broadcast_to(v,(2,NYD))
    stencil(vel,thick,cor,mask,xh.at[0],xh.at[1],yh.at[0],yh.at[1],ss,put,put_fac)
V=pl.BlockSpec(memory_space=pltpu.VMEM); SM=pl.BlockSpec(memory_space=pltpu.SMEM)


V = pl.BlockSpec(memory_space=pltpu.VMEM)
ANY = pl.BlockSpec(memory_space=pl.ANY)
SM = pl.BlockSpec(memory_space=pltpu.SMEM)


def pack_edge_kernel(pos, stress_hbm, tile_hbm, cell_hbm, weight_hbm, vel_hbm, mask_hbm,
                     main_hbm, tail_hbm, xe_hbm, ye_hbm,
                     stress, tile, cell, weight, vel, mask, main, tail, xe, ye, key_s, val_s, tr_s, isem, osem):
    pairs = ((tile_hbm, tile), (cell_hbm, cell), (weight_hbm, weight), (stress_hbm, stress), (vel_hbm, vel), (mask_hbm, mask))
    loads = [pltpu.make_async_copy(a, b, isem.at[k]) for k, (a, b) in enumerate(pairs)]
    for copy in loads:
        copy.start()
    for copy in loads[:4]:
        copy.wait()
    pack_kernel(pos, stress, tile, cell, weight, main, tail, key_s, val_s, tr_s)
    outs = ((main, main_hbm), (tail, tail_hbm), (xe, xe_hbm), (ye, ye_hbm))
    stores = [pltpu.make_async_copy(a, b, osem.at[k]) for k, (a, b) in enumerate(outs)]
    for copy in stores[:2]:
        copy.start()
    for copy in loads[4:]:
        copy.wait()
    edges(vel, mask, xe, ye)
    for copy in stores[2:]:
        copy.start()
    for copy in stores:
        copy.wait()


def pack_edge(pos, stress, tile, cell, weight, vel, mask):
    D = pltpu.SemaphoreType.DMA
    S = jax.ShapeDtypeStruct
    args = (stress.reshape(2, 72, 128).transpose(1, 0, 2), tile.reshape(72, 128), cell.reshape(72, 128),
            weight.reshape(72, 128), vel, mask)
    outs = (S((256, 4, 128), F32), S((256, 1, 128), F32), S((2, 2, 8, NYD), F32), S((3, 2, 2, 8, 128), F32))
    return pl.pallas_call(
        pack_edge_kernel,
        out_shape=outs,
        in_specs=[SM] + [ANY] * 6,
        out_specs=(ANY,) * 4,
        scratch_shapes=[pltpu.VMEM(a.shape, a.dtype) for a in args + outs] + [
            pltpu.VMEM((72, 128), I32), pltpu.VMEM((3, 72, 128), F32), pltpu.VMEM((128, 128), F32), D((6,)), D((4,))],
        compiler_params=pltpu.CompilerParams(vmem_limit_bytes=60 << 20),
    )(pos, *args)


def coords(d):
    return d // 128, d // 8 % 16, d % 8


def exchange_kernel(main, tail, xe, ye, rec, rtail, xh, yh, lsem, ssem, rsem, xs, xr, ys, yr):
    comp, ox, oy = lax.axis_index("comp"), lax.axis_index("ox"), lax.axis_index("oy")
    me = comp * 128 + ox * 8 + oy
    p = comp * 16 + ox
    barrier = pltpu.get_barrier_semaphore()

    def greet(i, carry):
        pl.semaphore_signal(barrier, inc=1, device_id=coords((me + i) % 256), device_id_type=MESH)
        return carry

    lax.fori_loop(1, 256, greet, 0)
    own = [
        pltpu.make_async_copy(main.at[me], rec.at[me], lsem.at[0]),
        pltpu.make_async_copy(tail.at[me], rtail.at[me], lsem.at[1]),
    ]
    for copy in own:
        copy.start()
    pl.semaphore_wait(barrier, 255)

    def remote(src, dst, ss, rs, pp, oyy):
        return pltpu.make_async_remote_copy(
            src_ref=src, dst_ref=dst, send_sem=ss, recv_sem=rs,
            device_id=(pp // 16, pp % 16, oyy), device_id_type=MESH)

    west, east = (p + 31) % 32, (p + 1) % 32
    x_low = remote(xe.at[0], xh.at[1], xs.at[0], xr.at[1], west, oy)
    x_high = remote(xe.at[1], xh.at[0], xs.at[1], xr.at[0], east, oy)
    y_low = remote(ye.at[0], yh.at[1], ys.at[0], yr.at[1], p, (oy + 7) % 8)
    y_high = remote(ye.at[1], yh.at[0], ys.at[1], yr.at[0], p, (oy + 1) % 8)
    fold = remote(ye.at[2], yh.at[1], ys.at[2], yr.at[1], 31 - p, oy)
    x_low.start()
    x_high.start()

    @pl.when(oy > 0)
    def _():
        y_low.start()

    @pl.when(oy < 7)
    def _():
        y_high.start()

    @pl.when(oy == 7)
    def _():
        fold.start()

    def send(i, carry):
        d = (me + i) % 256
        dev = coords(d)
        pltpu.make_async_remote_copy(
            src_ref=main.at[d], dst_ref=rec.at[me], send_sem=ssem.at[0], recv_sem=rsem.at[0],
            device_id=dev, device_id_type=MESH).start()
        pltpu.make_async_remote_copy(
            src_ref=tail.at[d], dst_ref=rtail.at[me], send_sem=ssem.at[1], recv_sem=rsem.at[1],
            device_id=dev, device_id_type=MESH).start()
        return carry

    lax.fori_loop(1, 256, send, 0)
    for copy in own:
        copy.wait()
    x_low.wait()
    x_high.wait()

    @pl.when(oy > 0)
    def _():
        y_low.wait_send()
        pltpu.make_async_copy(ye.at[1], yh.at[0], yr.at[0]).wait()

    @pl.when(oy < 7)
    def _():
        y_high.wait_send()

    @pl.when(oy == 7)
    def _():
        fold.wait_send()

    pltpu.make_async_copy(ye.at[0], yh.at[1], yr.at[1]).wait()
    n = pl.ds(0, 255)
    pltpu.make_async_copy(main.at[n], rec.at[n], ssem.at[0]).wait()
    pltpu.make_async_copy(tail.at[n], rtail.at[n], ssem.at[1]).wait()
    pltpu.make_async_copy(main.at[n], rec.at[n], rsem.at[0]).wait()
    pltpu.make_async_copy(tail.at[n], rtail.at[n], rsem.at[1]).wait()


def exchange(main, tail, xe, ye):
    shapes = [jax.ShapeDtypeStruct(a.shape, a.dtype) for a in (main, tail, xe)]
    shapes.append(jax.ShapeDtypeStruct((2, 2, 2, 8, 128), F32))
    D = pltpu.SemaphoreType.DMA
    return pl.pallas_call(
        exchange_kernel,
        out_shape=tuple(shapes),
        in_specs=[ANY] * 4,
        out_specs=(ANY,) * 4,
        scratch_shapes=[D((2,)), D((2,)), D((2,)), D((2,)), D((2,)), D((3,)), D((2,))],
        compiler_params=pltpu.CompilerParams(collective_id=0, has_side_effects=True),
    )(main, tail, xe, ye)


ROWS = 15


def finish_kernel(pos, rec_hbm, rtail_hbm, axes_hbm, vel_hbm, thick_hbm, cor_hbm, mask_hbm, xh_hbm, yh_hbm, out_hbm,
                  vel, thick, cor, mask, xh, yh, rec, rtail, ent, mm_v, mm_s, amat0, amat1, bmat0, bmat1, jobs, surf, flat, step, axes, fac, sem, isem, osem, lsem):
    first = [
        pltpu.make_async_copy(rec_hbm, rec, isem.at[3]),
        pltpu.make_async_copy(rtail_hbm, rtail, isem.at[4]),
    ]
    for copy in first:
        copy.start()
    pairs = ((axes_hbm, axes), (vel_hbm, vel), (thick_hbm, thick), (cor_hbm, cor), (mask_hbm, mask), (xh_hbm, xh), (yh_hbm, yh))
    loads = [pltpu.make_async_copy(a, b, lsem.at[k]) for k, (a, b) in enumerate(pairs)]
    for copy in loads:
        copy.start()
    for copy in first:
        copy.wait()
    unpack_prepare(rec, rtail, ent, mm_v)
    copy = pltpu.make_async_copy(mm_v, mm_s, sem)
    copy.start()
    surf[...] = jnp.zeros_like(surf)
    copy.wait()
    unpack_chunks(ent, mm_s, surf, amat0, amat1, bmat0, bmat1, jobs)
    for c in range(3):
        for h in range(2):
            flat[pl.ds(h, 216, stride=2), c, :] = surf[c, 0:216, 128 * h:128 * h + 128]
    for copy in loads:
        copy.wait()
    stencil_kernel(pos, vel, thick, cor, mask, xh, yh, step, fac)

    def row(x):
        r, o = 405 * x // 128, 405 * x % 128
        lane = lax.broadcasted_iota(I32, (4, 128), 1)
        t = [pltpu.roll(flat[r + k], (128 - o) % 128, 1) for k in range(5)]
        cut = lane < 128 - o
        for q in range(4):
            w = min(128, NYD - 128 * q)
            s = jnp.where(cut, t[q], t[q + 1])
            cols = pl.ds(128 * q, w)
            total = jnp.zeros((2, w), F32)
            for c in range(3):
                total += axes[c, x, :, cols] * jnp.broadcast_to(s[c:c + 1, :w], (2, w))
            total = total * fac[x, :, cols]
            for i in range(2):
                step[i, x, 0:1, cols] += total[i:i + 1, :]

    def out_copy(g):
        rows = pl.ds(g * ROWS, ROWS)
        return pltpu.make_async_copy(step.at[:, rows], out_hbm.at[:, rows], osem.at[g])

    def group(g, carry):
        def one(k, carry):
            row(g * ROWS + k)
            return carry

        lax.fori_loop(0, ROWS, one, 0, unroll=3)
        out_copy(g).start()
        return carry

    lax.fori_loop(0, NXD // ROWS, group, 0)

    def drain(g, carry):
        out_copy(g).wait()
        return carry

    lax.fori_loop(0, NXD // ROWS, drain, 0)


def finish(pos, rec, rtail, axes, vel, thick, cor, mask, xh, yh):
    D = pltpu.SemaphoreType.DMA
    return pl.pallas_call(
        finish_kernel,
        out_shape=jax.ShapeDtypeStruct((2, NXD, 8, NYD), F32),
        in_specs=[SM] + [ANY] * 9,
        out_specs=ANY,
        scratch_shapes=[pltpu.VMEM(a.shape, a.dtype) for a in (vel, thick, cor, mask, xh, yh)] + [
            pltpu.VMEM((256, 4, 128), F32), pltpu.VMEM((256, 1, 128), F32),
            pltpu.VMEM((8, 288, 128), F32), pltpu.VMEM((8, 256), I32), pltpu.SMEM((8, 256), I32),
            pltpu.VMEM((6 * W, SL * 256), BF), pltpu.VMEM((6 * W, SL * 256), BF),
            pltpu.VMEM((256, SL * 256), BF), pltpu.VMEM((256, SL * 256), BF), pltpu.SMEM((2, 64), I32),
            pltpu.VMEM((3, AR, 256), F32), pltpu.VMEM((432, 4, 128), F32),
            pltpu.VMEM((2, NXD, 8, NYD), F32), pltpu.VMEM((3, NXD, 2, NYD), F32), pltpu.VMEM((NXD, 2, NYD), F32),
            D, D((5,)), D((NXD // ROWS,)), D((7,)),
        ],
        compiler_params=pltpu.CompilerParams(vmem_limit_bytes=60 << 20),
    )(pos, rec, rtail, axes, vel, thick, cor, mask, xh, yh)


def shards(atmos_stress, route_tile, route_cell, route_weight, velocity, thickness, coriolis, ocean_axes, ocean_mask):
    vel = velocity.transpose(0, 2, 1, 3)
    pos = jnp.stack([lax.axis_index("comp"), lax.axis_index("ox"), lax.axis_index("oy")]).astype(I32)
    main, tail, xe, ye = pack_edge(pos, atmos_stress, route_tile, route_cell, route_weight, vel, ocean_mask)
    rec, rtail, xh, yh = exchange(main, tail, xe, ye)
    out = finish(pos, rec, rtail, ocean_axes.transpose(1, 2, 0, 3), vel, thickness.transpose(1, 0, 2), coriolis,
                 ocean_mask, xh, yh)
    return out.transpose(0, 2, 1, 3)


def solution(mesh):
    return jax.shard_map(
        shards,
        mesh=mesh,
        in_specs=(
            P(None, ("comp", "ox", "oy")),
            P(("comp", "ox", "oy"), None),
            P(("comp", "ox", "oy")),
            P(("comp", "ox", "oy")),
            P(None, None, ("comp", "ox"), "oy"),
            P(None, ("comp", "ox"), "oy"),
            P(("comp", "ox"), "oy"),
            P(None, None, ("comp", "ox"), "oy"),
            P(("comp", "ox"), "oy"),
        ),
        out_specs=P(None, None, ("comp", "ox"), "oy"),
        check_vma=False,
    )
```

```python
import math

import jax
import jax.numpy as jnp
from jax import lax
from jax.experimental import pallas as pl
from jax.experimental.pallas import tpu as pltpu
from jax.sharding import PartitionSpec as P

BF = jnp.bfloat16
F32 = jnp.float32
I32 = jnp.int32
MESH = pl.DeviceIdType.MESH
LOGICAL = pl.DeviceIdType.LOGICAL
FN=[[1,0,0],[0,1,0],[-1,0,0],[0,-1,0],[0,0,1],[0,0,-1]]
FA=[[0,1,0],[-1,0,0],[0,-1,0],[1,0,0],[0,1,0],[0,1,0]]
FB=[[0,0,1],[0,0,1],[0,0,1],[0,0,1],[-1,0,0],[1,0,0]]

def tan_small(t):
    u=t*t
    s=t*(1.0+u*(-1/6.0+u*(1/120.0+u*(-1/5040.0+u*(1/362880.0)))))
    c=1.0+u*(-0.5+u*(1/24.0+u*(-1/720.0+u*(1/40320.0+u*(-1/3628800.0)))))
    return s/c

def pack_kernel(pos_ref, stress_ref, tile_ref, cell_ref, weight_ref, out_ref, tout_ref, key_s, val_s, tr_s):
    comp=pos_ref[0]; ox=pos_ref[1]; oy=pos_ref[2]
    for f in range(3):
        rows=pl.ds(24*f,24)
        sub=lax.broadcasted_iota(I32,(24,128),0); lane=lax.broadcasted_iota(I32,(24,128),1)
        crow=ox*48+2*sub+lane//64
        ccol=oy*64+lane%64
        p=tan_small((crow.astype(F32)+0.5)*(0.5*math.pi/768)-0.25*math.pi)
        q=tan_small((ccol.astype(F32)+0.5)*(0.5*math.pi/512)-0.25*math.pi)
        pp=1.0+p*p; qq=1.0+q*q; rs=lax.rsqrt(pp+q*q)
        w=weight_ref[rows,:]*rs
        u=stress_ref[rows,0,:]*w*lax.rsqrt(qq)
        v=stress_ref[rows,1,:]*w*lax.rsqrt(pp)
        N=-(p*u+q*v); A=qq*u-p*q*v; B=pp*v-p*q*u
        for c in range(3):
            def coef(T): return jnp.where(comp==0,float(T[f][c]),float(T[f+3][c])).astype(F32)
            val_s[c,rows,:]=N*coef(FN)+A*coef(FA)+B*coef(FB)
    key_s[...]=tile_ref[...]*65536+cell_ref[...]
    tid=lax.broadcasted_iota(I32,(256,128),0)
    def cnt(r,acc):
        rows=tile_ref[pl.ds(pl.multiple_of(8*r,8),8),:]
        for k in range(8):
            acc=acc+jnp.where(jnp.broadcast_to(rows[k:k+1,:],(256,128))<tid,1.0,0.0)
        return acc
    acc=lax.fori_loop(0,9,cnt,jnp.zeros((256,128),F32))
    start=jnp.sum(acc,axis=1,keepdims=True)
    keys=[key_s[pl.ds(8*i,8),:] for i in range(9)]+[jnp.full((8,128),2**31-1,I32)]*7
    vals=[[val_s[c,pl.ds(8*i,8),:] for i in range(9)]+[jnp.zeros((8,128),F32)]*7 for c in range(3)]
    lane=lax.broadcasted_iota(I32,(8,128),1); sub=lax.broadcasted_iota(I32,(8,128),0)
    arrs=[keys]+vals
    def bitmask(b):
        if b<3: return (sub>>b)&1
        if b<7: return [bool((i>>(b-3))&1) for i in range(16)]
        return (lane>>(b-7))&1
    for kk in range(1,15):
        for j in reversed(range(kk)):
            dirbits=bitmask(kk) if kk<14 else [False]*16
            if 3<=j<7:
                new=[[None]*16 for _ in arrs]
                for i in range(16):
                    if (i>>(j-3))&1: continue
                    h=i|(1<<(j-3))
                    a,b=arrs[0][i],arrs[0][h]
                    gt=a>b
                    if isinstance(dirbits,list):
                        swap=(b>a) if dirbits[i] else gt
                    else:
                        swap=jnp.where(dirbits==1,b-a,a-b)>0
                    for n in range(4):
                        x,y=arrs[n][i],arrs[n][h]
                        new[n][i]=jnp.where(swap,y,x); new[n][h]=jnp.where(swap,x,y)
                arrs=new
            else:
                bit=bitmask(j)
                if isinstance(dirbits,list): sgn=None
                new=[[None]*16 for _ in arrs]
                if j<3:
                    d=1<<j
                    part=lambda x: jnp.where(bit==1,pltpu.roll(x,d,0),pltpu.roll(x,8-d,0)) if d<4 else pltpu.roll(x,4,0)
                else:
                    d=1<<(j-7)
                    if d==64: part=lambda x: pltpu.roll(x,64,1)
                    else: part=lambda x: jnp.take_along_axis(x,lane^d,axis=1,mode="promise_in_bounds")
                for i in range(16):
                    k=arrs[0][i]; pk=part(k)
                    if isinstance(dirbits,list): flip=bit^(1 if dirbits[i] else 0)
                    else: flip=bit^dirbits
                    take=jnp.where(flip==1,pk-k,k-pk)>0
                    new[0][i]=jnp.where(take,pk,k)
                    for n in range(1,4):
                        x=arrs[n][i]
                        new[n][i]=jnp.where(take,part(x),x)
                arrs=new
    turned=[None]*4
    for n in range(4):
        for v in range(16):
            x=arrs[n][v]
            if n==0: x=(x&65535).astype(F32)
            tr_s[pl.ds(8*v,8),:]=x
        turned[3 if n==0 else n-1]=tr_s[...].T
    table=jnp.concatenate(turned,axis=1)
    p0=table.astype(BF); d0=table-p0.astype(F32)
    p1=d0.astype(BF); p2=(d0-p1.astype(F32)).astype(BF)
    lane=lax.broadcasted_iota(I32,(256,128),1).astype(F32)
    start=jnp.broadcast_to(start,(256,128))
    row=jnp.floor(start*(1.0/128)); off=start-128.0*row
    last=lax.broadcasted_iota(I32,(256,128),0)==255
    left=jnp.where(last,9216.0,pltpu.roll(start,255,0))-start
    got=[]
    for k in range(3):
        pick=jnp.where(lane==row+float(k),1.0,0.0).astype(BF)
        got.append(sum(jnp.dot(pick,q,preferred_element_type=F32) for q in (p0,p1,p2)))
    at=(lane+off).astype(I32)&127
    inlo=lane+off<128.0
    tl=jnp.zeros((256,128),F32)
    for c in range(4):
        y0,y1,y2=[jnp.take_along_axis(g[:,128*c:128*c+128],at,axis=1,mode="promise_in_bounds") for g in got]
        fill=-1.0 if c==3 else 0.0
        out_ref[:,c,:]=jnp.where(lane<left,jnp.where(inlo,y0,y1),fill)
        g=jnp.where(lane+128.0<left,jnp.where(inlo,y1,y2),fill)
        if c: g=pltpu.roll(g,16*c,1)
        tl=jnp.where((lane>=16.0*c)&(lane<16.0*c+16.0),g,tl)
    tout_ref[:,0,:]=tl

W=80; SL=8; AR=304
def unpack_prepare(rec_ref, tail_ref, ent, mm_v):
    lane=lax.broadcasted_iota(I32,(256,128),1)
    tail=tail_ref[:,0,:]
    cellm=rec_ref[:,3,:]
    cellt=pltpu.roll(tail,80,1)
    n=jnp.sum(jnp.where(cellm>=0,1.0,0.0),axis=1,keepdims=True)+jnp.sum(jnp.where((cellt>=0)&(lane<16),1.0,0.0),axis=1,keepdims=True)
    S=jnp.maximum(jnp.max(n),1.0)
    def where_from(l):
        f=jnp.minimum(jnp.floor((l.astype(F32)*n+0.5)/S),143.0)
        g=jnp.minimum(jnp.floor(((l-1).astype(F32)*n+0.5)/S),143.0)
        return f,((f!=g)|(l==0))&(l.astype(F32)<S)&(n>0)
    fm,okm=where_from(lane)
    ft,okt=where_from(lane%16+128)
    fmi=jnp.clip(fm.astype(I32),0,127); fti=jnp.clip(ft.astype(I32),0,143)
    lo_i=jnp.minimum(fti,127)
    intail=fti>=128
    for c in (3,0,1,2):
        main=rec_ref[:,c,:]
        t=pltpu.roll(tail,(128-16*c)%128,1) if c else tail
        m2=jnp.take_along_axis(main,fmi,axis=1,mode="promise_in_bounds")
        ta=jnp.take_along_axis(main,lo_i,axis=1,mode="promise_in_bounds")
        tb=jnp.take_along_axis(t,jnp.where(intail,fti-128,0),axis=1,mode="promise_in_bounds")
        t2=jnp.where(intail,tb,ta)
        if c==3:
            m2=jnp.where(okm,m2,-1.0); t2=jnp.where(okt,t2,-1.0)
            for q,x in enumerate((m2,t2)):
                a=jnp.floor((x+0.5)*(1/256.0))
                mn=jnp.min(jnp.where(x>=0,a,999.0),axis=0,keepdims=True)
                mx=jnp.max(a,axis=0,keepdims=True)
                mm_v[pl.ds(0,1),pl.ds(128*q,128)]=mn.astype(I32)
                mm_v[pl.ds(1,1),pl.ds(128*q,128)]=mx.astype(I32)
        for x,r0,nr in ((m2,0,128),(t2,128,16)):
          for hh in range(2):
            y=x[128*hh:128*hh+128].T[:nr]
            rows=pl.ds(144*hh+r0,nr)
            if c==3:
                a=jnp.floor((y+0.5)*(1/256.0))
                ent[6,rows,:]=a
                ent[7,rows,:]=y-256.0*a
            else:
                h=y.astype(BF).astype(F32)
                ent[2*c,rows,:]=h
                ent[2*c+1,rows,:]=y-h
def unpack_chunks(ent, mm_s, surf, amat0, amat1, bmat0, bmat1, jobs):
    ib=lax.broadcasted_iota(I32,(256,128),0).astype(F32).astype(BF)
    ia=lax.broadcasted_iota(I32,(W,128),0).astype(F32).astype(BF)
    one=jnp.ones((256,128),BF); zb=jnp.zeros((256,128),BF); za=jnp.zeros((W,128),BF)
    def row(k,j,h): return jnp.broadcast_to(ent[k,pl.ds(144*h+j,1),:],(16,128))
    def chunk(i,n):
        lo=mm_s[0,i*SL]; hi=mm_s[1,i*SL]
        for q in range(1,SL):
            lo=jnp.minimum(lo,mm_s[0,i*SL+q]); hi=jnp.maximum(hi,mm_s[1,i*SL+q])
        base=(lo//8)*8
        def add(w,n):
            jobs[0,n]=i
            jobs[1,n]=base+w*W
            return n+1
        return lax.fori_loop(0,jnp.where(hi>=0,(hi-base)//W+1,0),add,n)
    n=lax.fori_loop(0,144//SL,chunk,0)
    for k in range(3):
        jobs[0,n+k]=0
        jobs[1,n+k]=AR-W
    def make(k,amat,bmat):
        i=jobs[0,k]; a0=jobs[1,k].astype(F32)
        for j in range(SL):
            for h in range(2):
                cols=pl.ds((2*j+h)*128,128)
                bb=row(7,i*SL+j,h).astype(BF)
                bmat[:,cols]=jnp.where(ib==jnp.tile(bb,(16,1)),one,zb)
                ab=(row(6,i*SL+j,h)-a0).astype(BF)
                m=ia==jnp.tile(ab,(W//16,1))
                for q in range(6):
                    v=row(q,i*SL+j,h).astype(BF)
                    amat[pl.ds(q*W,W),cols]=jnp.where(m,jnp.tile(v,(W//16,1)),za)
    def add_product(k,amat,bmat):
        a0=pl.multiple_of(jobs[1,k],8)
        r=lax.dot_general(amat[...],bmat[...],(((1,),(1,)),((),())),preferred_element_type=F32)
        for c in range(3):
            surf[c,pl.ds(a0,W),:]+=r[2*c*W:(2*c+1)*W]+r[(2*c+1)*W:(2*c+2)*W]
    make(0,amat0,bmat0)
    def pair(t,carry):
        make(2*t+1,amat1,bmat1)
        add_product(2*t,amat0,bmat0)
        make(2*t+2,amat0,bmat0)
        add_product(2*t+1,amat1,bmat1)
        return carry
    lax.fori_loop(0,(n+1)//2,pair,0)
NXD,NYD=135,405

def edges(vel, mask_ref, xe_ref, ye_ref):
    for s,x in ((0,0),(1,NXD-1)):
        M=mask_ref[0:8,:] if s==0 else mask_ref[NXD-8:NXD,:]
        j=0 if s==0 else 7
        m=jnp.broadcast_to(M[j:j+1,:],(8,NYD)).astype(F32)
        for c in range(2): xe_ref[s,c]=vel[c,x]*m
    ye_ref[...]=jnp.zeros_like(ye_ref)
    lane=lax.broadcasted_iota(I32,(8,128),1)
    def block(x0,first,M):
        ma=M[:,0:1]; mb=M[:,NYD-1:NYD]
        static=isinstance(x0,int)
        q=x0//128 if static else 0
        o=x0%128
        for c in range(2):
            lo=jnp.zeros((8,128),F32); hi=lo; fold=lo
            for j in range(first,8):
                v=vel[c,x0+j]
                a=v[:,0:1]*ma[j:j+1,:]
                b=v[:,NYD-1:NYD]*mb[j:j+1,:]
                lo=jnp.where(lane==j,a,lo); hi=jnp.where(lane==j,b,hi); fold=jnp.where(lane==7-j,-b,fold)
            f=pltpu.roll(fold,(127-x0)%128 if static else (127-x0),1)
            lo=pltpu.roll(lo,o,1); hi=pltpu.roll(hi,o,1)
            if static and x0==127:
                ye_ref[0,c,1]=jnp.where(lane<7,lo,0.0); ye_ref[1,c,1]=jnp.where(lane<7,hi,0.0)
                ye_ref[2,c,0]+=f
            elif static and x0==0:
                ye_ref[0,c,0]+=lo; ye_ref[1,c,0]+=hi
                ye_ref[2,c,1]+=jnp.where(lane<7,f,0.0); ye_ref[2,c,0]+=jnp.where(lane==127,f,0.0)
            else:
                ye_ref[0,c,0]+=lo; ye_ref[1,c,0]+=hi; ye_ref[2,c,0]+=f
    def rows(x0): return mask_ref[pl.ds(x0,8),:].astype(F32)
    block(0,0,rows(0))
    def body(i,carry):
        x0=pl.multiple_of(8*i,8)
        block(x0,0,rows(x0))
        return carry
    lax.fori_loop(1,16,body,0)
    block(127,1,mask_ref[NXD-8:NXD,:].astype(F32))

def stencil(vel, thick, cor, mask, xlo, xhi, ylo, yhi, south_scale, put, put_fac):
    sub=lax.broadcasted_iota(I32,(8,NYD),0)
    def mrow(M,j): return jnp.broadcast_to(M[j:j+1,:],(8,NYD))
    def rows8(ref,x0): return ref[pl.ds(x0,8),:].astype(F32)
    M_end=mask[NXD-8:NXD,:].astype(F32)[1:8]; C_end=cor[NXD-8:NXD,:][1:8]
    def block(x0,n,prev,cur,last):
        M=M_end if last else rows8(mask,x0); C=C_end if last else rows8(cor,x0)
        if not last:
            Mn=M_end if isinstance(x0,int) else rows8(mask,pl.multiple_of(x0+8,8))
        q=x0//128 if isinstance(x0,int) else 0
        o=(128-x0%128)%128
        lo=[jnp.where(south_scale>0,pltpu.roll(ylo[c,q],o,1),0.0) for c in range(2)]
        hi=[pltpu.roll(yhi[c,q],o,1) for c in range(2)]
        for j in range(n):
            x=x0+j
            th=thick[x]; inv=1.0/th
            g=0.6/(th+pltpu.roll(th,7,0))
            m1=mrow(M,j); cj=mrow(C,j)
            put_fac(x,M[j:j+1,:]*inv[0:1,:])
            if last and j==n-1: nx=[xhi[c] for c in range(2)]
            else:
                mn=mrow(M,j+1) if j+1<n else mrow(Mn,0)
                nx=[vel[c,x+1]*mn for c in range(2)]
            for c in range(2):
                m=cur[c]
                north=jnp.concatenate([m[:,1:],hi[c][:,j:j+1]],axis=1)
                south=jnp.concatenate([lo[c][:,j:j+1],m[:,:-1]],axis=1)
                lap=(nx[c]+prev[c])+(north+south)-4.0*m
                D=jnp.where(sub==7,0.1*m,g*(m-pltpu.roll(m,7,0)))
                ab=jnp.where(sub==0,0.0,pltpu.roll(D,1,0))
                turn=cj*cur[1] if c==0 else -cj*cur[0]
                put(c,x,(m+turn+0.2*lap+(ab-D)*inv)*m1)
            prev,cur=cur,nx
        return prev,cur
    m0=jnp.broadcast_to(rows8(mask,0)[0:1,:],(8,NYD))
    prev=[xlo[c] for c in range(2)]; cur=[vel[c,0]*m0 for c in range(2)]
    def body(i,st):
        p,c=block(pl.multiple_of(8*i,8),8,list(st[0]),list(st[1]),False)
        return tuple(p),tuple(c)
    st=lax.fori_loop(0,15,body,(tuple(prev),tuple(cur)))
    st=block(120,8,list(st[0]),list(st[1]),False)
    block(128,7,list(st[0]),list(st[1]),True)

def stencil_kernel(pos_ref,vel,thick,cor,mask,xh,yh,out,fac):
    ss=jnp.where(pos_ref[2]==0,0.0,1.0).astype(F32)
    def put(c,x,v): out[c,x]=v
    def put_fac(x,v): fac[x]=jnp.broadcast_to(v,(2,NYD))
    stencil(vel,thick,cor,mask,xh.at[0],xh.at[1],yh.at[0],yh.at[1],ss,put,put_fac)
V=pl.BlockSpec(memory_space=pltpu.VMEM); SM=pl.BlockSpec(memory_space=pltpu.SMEM)


V = pl.BlockSpec(memory_space=pltpu.VMEM)
ANY = pl.BlockSpec(memory_space=pl.ANY)
SM = pl.BlockSpec(memory_space=pltpu.SMEM)


def pack_edge_kernel(pos, stress_hbm, tile_hbm, cell_hbm, weight_hbm, vel_hbm, mask_hbm,
                     main_hbm, tail_hbm, xe_hbm, ye_hbm,
                     stress, tile, cell, weight, vel, mask, main, tail, xe, ye, key_s, val_s, tr_s, isem, osem):
    pairs = ((tile_hbm, tile), (cell_hbm, cell), (weight_hbm, weight), (stress_hbm, stress), (vel_hbm, vel), (mask_hbm, mask))
    loads = [pltpu.make_async_copy(a, b, isem.at[k]) for k, (a, b) in enumerate(pairs)]
    for copy in loads:
        copy.start()
    for copy in loads[:4]:
        copy.wait()
    pack_kernel(pos, stress, tile, cell, weight, main, tail, key_s, val_s, tr_s)
    outs = ((main, main_hbm), (tail, tail_hbm), (xe, xe_hbm), (ye, ye_hbm))
    stores = [pltpu.make_async_copy(a, b, osem.at[k]) for k, (a, b) in enumerate(outs)]
    for copy in stores[:2]:
        copy.start()
    for copy in loads[4:]:
        copy.wait()
    edges(vel, mask, xe, ye)
    for copy in stores[2:]:
        copy.start()
    for copy in stores:
        copy.wait()


def pack_edge(pos, stress, tile, cell, weight, vel, mask):
    D = pltpu.SemaphoreType.DMA
    S = jax.ShapeDtypeStruct
    args = (stress.reshape(2, 72, 128).transpose(1, 0, 2), tile.reshape(72, 128), cell.reshape(72, 128),
            weight.reshape(72, 128), vel, mask)
    outs = (S((256, 4, 128), F32), S((256, 1, 128), F32), S((2, 2, 8, NYD), F32), S((3, 2, 2, 8, 128), F32))
    return pl.pallas_call(
        pack_edge_kernel,
        out_shape=outs,
        in_specs=[SM] + [ANY] * 6,
        out_specs=(ANY,) * 4,
        scratch_shapes=[pltpu.VMEM(a.shape, a.dtype) for a in args + outs] + [
            pltpu.VMEM((72, 128), I32), pltpu.VMEM((3, 72, 128), F32), pltpu.VMEM((128, 128), F32), D((6,)), D((4,))],
        compiler_params=pltpu.CompilerParams(vmem_limit_bytes=60 << 20),
    )(pos, *args)


def exchange_kernel(main, tail, xe, ye, rec, rtail, xh, yh, lsem, ssem, rsem, xs, xr, ys, yr):
    comp, ox, oy = lax.axis_index("comp"), lax.axis_index("ox"), lax.axis_index("oy")
    me = comp * 128 + ox * 8 + oy
    p = comp * 16 + ox
    barrier = pltpu.get_barrier_semaphore()

    def greet(i, carry):
        for k in range(1, 6):
            pl.semaphore_signal(barrier, inc=1, device_id=(me + 5 * i + k) % 256, device_id_type=LOGICAL)
        return carry

    lax.fori_loop(0, 51, greet, 0)
    own = [
        pltpu.make_async_copy(main.at[me], rec.at[me], lsem.at[0]),
        pltpu.make_async_copy(tail.at[me], rtail.at[me], lsem.at[1]),
    ]
    for copy in own:
        copy.start()
    pl.semaphore_wait(barrier, 255)

    def remote(src, dst, ss, rs, pp, oyy):
        return pltpu.make_async_remote_copy(
            src_ref=src, dst_ref=dst, send_sem=ss, recv_sem=rs,
            device_id=(pp // 16, pp % 16, oyy), device_id_type=MESH)

    west, east = (p + 31) % 32, (p + 1) % 32
    x_low = remote(xe.at[0], xh.at[1], xs.at[0], xr.at[1], west, oy)
    x_high = remote(xe.at[1], xh.at[0], xs.at[1], xr.at[0], east, oy)
    y_low = remote(ye.at[0], yh.at[1], ys.at[0], yr.at[1], p, (oy + 7) % 8)
    y_high = remote(ye.at[1], yh.at[0], ys.at[1], yr.at[0], p, (oy + 1) % 8)
    fold = remote(ye.at[2], yh.at[1], ys.at[2], yr.at[1], 31 - p, oy)
    x_low.start()
    x_high.start()

    @pl.when(oy > 0)
    def _():
        y_low.start()

    @pl.when(oy < 7)
    def _():
        y_high.start()

    @pl.when(oy == 7)
    def _():
        fold.start()

    def send(i, carry):
        for k in range(1, 6):
            d = (me + 5 * i + k) % 256
            pltpu.make_async_remote_copy(
                src_ref=main.at[d], dst_ref=rec.at[me], send_sem=ssem.at[0], recv_sem=rsem.at[0],
                device_id=d, device_id_type=LOGICAL).start()
            pltpu.make_async_remote_copy(
                src_ref=tail.at[d], dst_ref=rtail.at[me], send_sem=ssem.at[1], recv_sem=rsem.at[1],
                device_id=d, device_id_type=LOGICAL).start()
        return carry

    lax.fori_loop(0, 51, send, 0)
    for copy in own:
        copy.wait()
    x_low.wait()
    x_high.wait()

    @pl.when(oy > 0)
    def _():
        y_low.wait_send()
        pltpu.make_async_copy(ye.at[1], yh.at[0], yr.at[0]).wait()

    @pl.when(oy < 7)
    def _():
        y_high.wait_send()

    @pl.when(oy == 7)
    def _():
        fold.wait_send()

    pltpu.make_async_copy(ye.at[0], yh.at[1], yr.at[1]).wait()
    n = pl.ds(0, 255)
    pltpu.make_async_copy(main.at[n], rec.at[n], ssem.at[0]).wait()
    pltpu.make_async_copy(tail.at[n], rtail.at[n], ssem.at[1]).wait()
    pltpu.make_async_copy(main.at[n], rec.at[n], rsem.at[0]).wait()
    pltpu.make_async_copy(tail.at[n], rtail.at[n], rsem.at[1]).wait()


def exchange(main, tail, xe, ye):
    shapes = [jax.ShapeDtypeStruct(a.shape, a.dtype) for a in (main, tail, xe)]
    shapes.append(jax.ShapeDtypeStruct((2, 2, 2, 8, 128), F32))
    D = pltpu.SemaphoreType.DMA
    return pl.pallas_call(
        exchange_kernel,
        out_shape=tuple(shapes),
        in_specs=[ANY] * 4,
        out_specs=(ANY,) * 4,
        scratch_shapes=[D((2,)), D((2,)), D((2,)), D((2,)), D((2,)), D((3,)), D((2,))],
        compiler_params=pltpu.CompilerParams(collective_id=0, has_side_effects=True),
    )(main, tail, xe, ye)


ROWS = 15


def finish_kernel(pos, rec_hbm, rtail_hbm, axes_hbm, vel_hbm, thick_hbm, cor_hbm, mask_hbm, xh_hbm, yh_hbm, out_hbm,
                  vel, thick, cor, mask, xh, yh, rec, rtail, ent, mm_v, mm_s, amat0, amat1, bmat0, bmat1, jobs, surf, flat, step, axes, fac, sem, isem, osem, lsem):
    first = [
        pltpu.make_async_copy(rec_hbm, rec, isem.at[3]),
        pltpu.make_async_copy(rtail_hbm, rtail, isem.at[4]),
    ]
    for copy in first:
        copy.start()
    pairs = ((axes_hbm, axes), (vel_hbm, vel), (thick_hbm, thick), (cor_hbm, cor), (mask_hbm, mask), (xh_hbm, xh), (yh_hbm, yh))
    loads = [pltpu.make_async_copy(a, b, lsem.at[k]) for k, (a, b) in enumerate(pairs)]
    for copy in loads:
        copy.start()
    for copy in first:
        copy.wait()
    unpack_prepare(rec, rtail, ent, mm_v)
    copy = pltpu.make_async_copy(mm_v, mm_s, sem)
    copy.start()
    surf[...] = jnp.zeros_like(surf)
    copy.wait()
    unpack_chunks(ent, mm_s, surf, amat0, amat1, bmat0, bmat1, jobs)
    for c in range(3):
        for h in range(2):
            flat[pl.ds(h, 216, stride=2), c, :] = surf[c, 0:216, 128 * h:128 * h + 128]
    for copy in loads:
        copy.wait()
    stencil_kernel(pos, vel, thick, cor, mask, xh, yh, step, fac)

    def row(x):
        r, o = 405 * x // 128, 405 * x % 128
        lane = lax.broadcasted_iota(I32, (4, 128), 1)
        t = [pltpu.roll(flat[r + k], (128 - o) % 128, 1) for k in range(5)]
        cut = lane < 128 - o
        for q in range(4):
            w = min(128, NYD - 128 * q)
            s = jnp.where(cut, t[q], t[q + 1])
            cols = pl.ds(128 * q, w)
            total = jnp.zeros((2, w), F32)
            for c in range(3):
                total += axes[c, x, :, cols] * jnp.broadcast_to(s[c:c + 1, :w], (2, w))
            total = total * fac[x, :, cols]
            for i in range(2):
                step[i, x, 0:1, cols] += total[i:i + 1, :]

    def out_copy(g):
        rows = pl.ds(g * ROWS, ROWS)
        return pltpu.make_async_copy(step.at[:, rows], out_hbm.at[:, rows], osem.at[g])

    def group(g, carry):
        def one(k, carry):
            row(g * ROWS + k)
            return carry

        lax.fori_loop(0, ROWS, one, 0, unroll=3)
        out_copy(g).start()
        return carry

    lax.fori_loop(0, NXD // ROWS, group, 0)

    def drain(g, carry):
        out_copy(g).wait()
        return carry

    lax.fori_loop(0, NXD // ROWS, drain, 0)


def finish(pos, rec, rtail, axes, vel, thick, cor, mask, xh, yh):
    D = pltpu.SemaphoreType.DMA
    return pl.pallas_call(
        finish_kernel,
        out_shape=jax.ShapeDtypeStruct((2, NXD, 8, NYD), F32),
        in_specs=[SM] + [ANY] * 9,
        out_specs=ANY,
        scratch_shapes=[pltpu.VMEM(a.shape, a.dtype) for a in (vel, thick, cor, mask, xh, yh)] + [
            pltpu.VMEM((256, 4, 128), F32), pltpu.VMEM((256, 1, 128), F32),
            pltpu.VMEM((8, 288, 128), F32), pltpu.VMEM((8, 256), I32), pltpu.SMEM((8, 256), I32),
            pltpu.VMEM((6 * W, SL * 256), BF), pltpu.VMEM((6 * W, SL * 256), BF),
            pltpu.VMEM((256, SL * 256), BF), pltpu.VMEM((256, SL * 256), BF), pltpu.SMEM((2, 64), I32),
            pltpu.VMEM((3, AR, 256), F32), pltpu.VMEM((432, 4, 128), F32),
            pltpu.VMEM((2, NXD, 8, NYD), F32), pltpu.VMEM((3, NXD, 2, NYD), F32), pltpu.VMEM((NXD, 2, NYD), F32),
            D, D((5,)), D((NXD // ROWS,)), D((7,)),
        ],
        compiler_params=pltpu.CompilerParams(vmem_limit_bytes=60 << 20),
    )(pos, rec, rtail, axes, vel, thick, cor, mask, xh, yh)


def shards(atmos_stress, route_tile, route_cell, route_weight, velocity, thickness, coriolis, ocean_axes, ocean_mask):
    vel = velocity.transpose(0, 2, 1, 3)
    pos = jnp.stack([lax.axis_index("comp"), lax.axis_index("ox"), lax.axis_index("oy")]).astype(I32)
    main, tail, xe, ye = pack_edge(pos, atmos_stress, route_tile, route_cell, route_weight, vel, ocean_mask)
    rec, rtail, xh, yh = exchange(main, tail, xe, ye)
    out = finish(pos, rec, rtail, ocean_axes.transpose(1, 2, 0, 3), vel, thickness.transpose(1, 0, 2), coriolis,
                 ocean_mask, xh, yh)
    return out.transpose(0, 2, 1, 3)


def solution(mesh):
    return jax.shard_map(
        shards,
        mesh=mesh,
        in_specs=(
            P(None, ("comp", "ox", "oy")),
            P(("comp", "ox", "oy"), None),
            P(("comp", "ox", "oy")),
            P(("comp", "ox", "oy")),
            P(None, None, ("comp", "ox"), "oy"),
            P(None, ("comp", "ox"), "oy"),
            P(("comp", "ox"), "oy"),
            P(None, None, ("comp", "ox"), "oy"),
            P(("comp", "ox"), "oy"),
        ),
        out_specs=P(None, None, ("comp", "ox"), "oy"),
        check_vma=False,
    )
```
